128 devices in a mesh: elem: 16 (over z_hi, y, core), mode: 8 (over x, z_lo).
Axes of the slice: x: 4, y: 4, z: 4 (z_hi: 2, z_lo: 2; z = z_hi * 2 + z_lo), core: 2. Of those that a mesh axis runs over, the one named last changes fastest.
Arguments:
- iterate: float32 [480, 16384], P('mode', 'elem'), may hold values from -0.75 to 0.75
- newton_residual: float32 [480, 16384], P('mode', 'elem'), may hold values from -6 to 6
- inverse_blocks: float32 [64, 16384], P(None, 'elem'), may hold values from -0.15 to 2
- basis_values: bfloat16 [1024, 480], replicated, may hold values from -4 to 4, as said below
- triple_blocks: bfloat16 [8, 60, 20160], P('mode', None, 'elem'), may hold values from -0.375 to 0.375
- block_columns: int32 [8, 4], P('mode'), may hold values from 0 to 7, as said below
- neighbour_ids: int32 [256, 6], P('elem'), may hold values from 0 to 15, as said below
Outputs:
- correction: float32 [480, 16384], P('mode', 'elem')
- linear_residual: float32 [480, 16384], P('mode', 'elem')
The draws below stay inside these ranges and needn't reach their ends.
Inputs may be any that keep to these rules, and one draw needn't show every extreme that they name: `neighbour_ids`: columns 0 to 3 give the neighbour across the -y, +y, -z, +z faces within the element's own block of 16 elements; columns 4 and 5 the neighbour across the -x and +x faces within the previous and the next block, cyclically. Neighbours are mutual across opposite faces. `block_columns`: row b names 4 different block columns; the first is b. `basis_values`: column 0 holds ones, the constant mode.
All inputs are finite; a program needn't handle non-finite values.
Results may differ from the reference program's by a relative error of at most 0.0039.
Values may be sent and summed in bfloat16 or wider, within the bound.
No kernel may reach another device: no remote copies, remote signals or barrier semaphores. Data moves between devices by JAX's collectives and lax.ppermute only.
A program may use at most 128 MiB of HBM per device.

```python
import math
import jax
import jax.numpy as jnp
import numpy as np
from jax import lax

P_SIZE = 480
K = 84
S = 1024
Q = 64
NB = 8
NNZB = 4
ITERS = 2
E_DEV = 16
MB = 60
NODES = 16384
N_ELEM = 16


def draw_basis_values(key, part):
    subkey = jax.random.fold_in(key, 11)
    values = jax.random.truncated_normal(subkey, -4.0, 4.0, (S, P_SIZE), jnp.float32)
    constant_column = jnp.arange(P_SIZE) == 0
    return jnp.where(constant_column[None, :], 1.0, values).astype(jnp.bfloat16)


def draw_inverse_blocks(key, part):
    node_total = E_DEV * Q * N_ELEM
    diagonal_key = jax.random.fold_in(key, 21)
    spread_key = jax.random.fold_in(key, 22)
    diagonal = jax.random.uniform(diagonal_key, (1, node_total), jnp.float32, 0.5, 1.5)
    spread = jax.random.truncated_normal(spread_key, -4.0, 4.0, (Q, node_total), jnp.float32) * (0.3 / math.sqrt(Q))
    source_rows = jnp.arange(Q)[:, None]
    target_rows = (jnp.arange(node_total) % Q)[None, :]
    return jnp.where(source_rows == target_rows, diagonal, spread).astype(jnp.float32)


def draw_block_columns(key, part):
    keys_list = jax.random.split(jax.random.fold_in(key, 5), NB)

    def one_row(subkey, row_index):
        others = jax.random.permutation(subkey, NB - 1) + 1
        return (row_index + others[:NNZB - 1]) % NB
    rest = jax.vmap(one_row)(keys_list, jnp.arange(NB))
    return jnp.concatenate([jnp.arange(NB)[:, None], rest], axis=1).astype(jnp.int32)


def draw_neighbour_ids(key, part):
    rows_across = E_DEV // 2
    keys_list = jax.random.split(jax.random.fold_in(key, 7), N_ELEM)
    orders = jax.vmap(lambda subkey: jax.random.permutation(subkey, E_DEV))(keys_list)
    places = jnp.argsort(orders, axis=1)
    blocks = jnp.arange(N_ELEM)[:, None]
    along_y = places // 2
    along_z = places % 2

    def lookup(block_index, y_index, z_index):
        return orders[block_index % N_ELEM, y_index % rows_across * 2 + z_index % 2]
    columns = [lookup(blocks, along_y - 1, along_z), lookup(blocks, along_y + 1, along_z), lookup(blocks, along_y, along_z - 1), lookup(blocks, along_y, along_z + 1), lookup(blocks - 1, along_y, along_z), lookup(blocks + 1, along_y, along_z)]
    return jnp.stack(columns, axis=-1).reshape(N_ELEM * E_DEV, 6).astype(jnp.int32)


def shard_levels(rng, dims, cuts, low, largest):
    factor_of = 1.0
    for position, parts in cuts:
        steps = jax.random.uniform(jax.random.fold_in(jax.random.fold_in(rng, 6), position), (parts,), jnp.float32, low / len(cuts), largest / len(cuts))
        factor_of = factor_of * jnp.repeat(jnp.exp(steps), dims[position] // parts).reshape((-1,) + (1,) * (len(dims) - 1 - position))
    return factor_of


def centred(rng, shape, scale, limit, shards=(), held_as=jnp.bfloat16):
    result = jax.random.normal(rng, shape, jnp.float32) * scale
    if len(shards) > 0:
        result = shard_levels(rng, shape, shards, -0.22, 0.18) * result
    return jnp.clip(result, min=-limit, max=limit).astype(held_as)


def setup_inputs(seed: int = 0) -> dict:
    key_of = jax.random.split(jax.random.key(seed), 8)
    iterate = centred(key_of[0], (P_SIZE, NODES), 0.05, 0.75, ((0, 8), (1, 16)), jnp.float32)
    newton_residual = centred(key_of[1], (P_SIZE, NODES), 1.0, 6.0, ((0, 8), (1, 16)), jnp.float32)
    inverse_blocks = draw_inverse_blocks(jax.random.fold_in(key_of[7], 71), 0)
    basis_values = draw_basis_values(jax.random.fold_in(key_of[7], 71), 0)
    triple_blocks = centred(key_of[4], (NB, MB, NNZB * MB * K), (NNZB * MB) ** -0.5, 0.375, ((0, 8), (2, 16)))
    block_columns = draw_block_columns(jax.random.fold_in(key_of[7], 71), 0)
    neighbour_ids = draw_neighbour_ids(jax.random.fold_in(key_of[7], 71), 0)
    return {"iterate": iterate, "newton_residual": newton_residual, "inverse_blocks": inverse_blocks, "basis_values": basis_values, "triple_blocks": triple_blocks, "block_columns": block_columns, "neighbour_ids": neighbour_ids}


GROWTH = 0.5
TIME_STEP = 0.03
LIFT_SCALE = 6.0
PENALTY = 3.0
RELAX_WEIGHT = 0.8
FACE_AXIS = (1, 1, 2, 2, 0, 0)
FACE_SIGN = (-1.0, 1.0, -1.0, 1.0, -1.0, 1.0)
FACE_OPPOSITE = (1, 0, 3, 2, 5, 4)

def line_derivative():
    inward = 1.0 / math.sqrt(5.0)
    points = np.array([-1.0, -inward, inward, 1.0])
    legendre = (5.0 * points ** 3 - 3.0 * points) / 2.0
    matrix = np.zeros((4, 4))
    for source in range(4):
        for target in range(4):
            if source != target:
                matrix[source, target] = legendre[source] / (legendre[target] * (points[source] - points[target]))
    matrix[0, 0] = -3.0
    matrix[3, 3] = 3.0
    return matrix

def direction_tables():
    line_matrix = line_derivative()
    identity = np.eye(4)
    singles = [np.kron(np.kron(line_matrix, identity), identity), np.kron(np.kron(identity, line_matrix), identity), np.kron(np.kron(identity, identity), line_matrix)]
    return [np.kron(np.eye(2), single).T.astype(np.float32) for single in singles]

def face_nodes():
    layout = np.arange(64).reshape(4, 4, 4)
    return np.stack([layout[:, 0, :].ravel(), layout[:, 3, :].ravel(), layout[:, :, 0].ravel(), layout[:, :, 3].ravel(), layout[0].ravel(), layout[3].ravel()])

def embed_table():
    nodes_list = face_nodes()
    table_out = np.zeros((96, 64), np.float32)
    for face_index in range(6):
        for within in range(16):
            table_out[face_index * 16 + within, nodes_list[face_index, within]] = 1.0
    return table_out

def volume_derivative(field, single):
    modes_count = field.shape[0]
    paired = field.reshape(-1, 128)
    return jnp.dot(paired, single, precision=lax.Precision.HIGHEST).reshape(modes_count, -1)

def apply_inverse(field, inverse_blocks):
    modes_count = field.shape[0]
    shaped = field.reshape(modes_count, -1, 64)
    inverse = inverse_blocks.reshape(64, -1, 64)
    return jnp.einsum('mer,req->meq', shaped, inverse, precision=lax.Precision.HIGHEST).reshape(modes_count, -1)

def own_traces(values, flux_fields, face_index, axis_index):
    nodes_list = face_nodes()
    return (values[:, :, nodes_list[face_index]], flux_fields[axis_index][:, :, nodes_list[face_index]])

def lift_terms(values, flux_fields, sources, near_ids, embed_matrix):
    pieces = []
    for face_index in range(6):
        own_values, own_fluxes = own_traces(values, flux_fields, face_index, FACE_AXIS[face_index])
        near_values = jnp.take(sources[face_index][0], near_ids[:, face_index], axis=1)
        near_fluxes = jnp.take(sources[face_index][1], near_ids[:, face_index], axis=1)
        pieces.append(LIFT_SCALE * (0.5 * FACE_SIGN[face_index] * (near_fluxes - own_fluxes) + PENALTY * (near_values - own_values)))
    joined = jnp.concatenate(pieces, axis=2)
    return jnp.einsum('mef,fq->meq', joined, embed_matrix, precision=lax.Precision.HIGHEST)

def neighbour_index(neighbour_ids):
    element_total = neighbour_ids.shape[0]
    owner_block = jnp.arange(element_total, dtype=jnp.int32) // E_DEV
    shifts = jnp.array([0, 0, 0, 0, -1, 1], dtype=jnp.int32)
    blocks = (owner_block[:, None] + shifts[None, :]) % N_ELEM
    return (blocks * E_DEV + neighbour_ids).astype(jnp.int32)

def triple_product(gradients, coeff_terms, triple_blocks, block_columns):
    block_width = triple_blocks.shape[1]
    nodes_count = gradients.shape[2]
    spread = coeff_terms.astype(jnp.float32)
    term_count = spread.shape[0]

    def one_row(operands):
        stored, columns = operands

        def add_block(stored_index, running):
            offset = (columns[stored_index] * block_width).astype(jnp.int32)
            picked = lax.dynamic_slice_in_dim(gradients, offset, block_width, 1)
            expanded = (picked.astype(jnp.float32)[:, :, None, :] * spread[None, None, :, :]).astype(jnp.bfloat16)
            expanded = expanded.reshape(3, block_width * term_count, nodes_count)
            weights = lax.dynamic_slice_in_dim(stored, (stored_index * block_width * term_count).astype(jnp.int32), block_width * term_count, 1)
            return running + jnp.einsum('il,cln->cin', weights.astype(jnp.float32), expanded.astype(jnp.float32))
        return lax.fori_loop(0, columns.shape[0], add_block, jnp.zeros((3, block_width, nodes_count), jnp.float32))
    per_row = lax.map(one_row, (triple_blocks, block_columns))
    return per_row.transpose(1, 0, 2, 3).reshape(3, -1, nodes_count).astype(jnp.bfloat16)

def apply_jacobian(iterate_now, coeff_terms, triple_blocks, block_columns, global_ids, tables, embed_matrix):
    modes_count = iterate_now.shape[0]
    gradients = jnp.stack([volume_derivative(iterate_now, single) for single in tables]).astype(jnp.bfloat16)
    fluxes = triple_product(gradients, coeff_terms, triple_blocks, block_columns)
    values = iterate_now.reshape(modes_count, -1, 64)
    flux_fields = fluxes.astype(jnp.float32).reshape(3, modes_count, -1, 64)
    sources = [own_traces(values, flux_fields, FACE_OPPOSITE[face_index], FACE_AXIS[face_index]) for face_index in range(6)]
    lifted = lift_terms(values, flux_fields, sources, global_ids, embed_matrix)
    divergence = lifted.reshape(modes_count, -1)
    for axis_index in range(3):
        divergence = divergence + volume_derivative(flux_fields[axis_index].reshape(modes_count, -1), tables[axis_index])
    return iterate_now - TIME_STEP * divergence

def reference(iterate, newton_residual, inverse_blocks, basis_values, triple_blocks, block_columns, neighbour_ids):
    tables = [jnp.asarray(single) for single in direction_tables()]
    embed_matrix = jnp.asarray(embed_table())
    global_ids = neighbour_index(neighbour_ids)
    low_state = iterate.astype(jnp.bfloat16)
    sampled = jnp.dot(basis_values, low_state, preferred_element_type=jnp.float32)
    growth = jnp.exp(GROWTH * sampled)
    leading = basis_values[:, :K].astype(jnp.float32)
    coeff_terms = (jnp.dot(leading.T, growth, precision=lax.Precision.HIGHEST) / S).astype(jnp.bfloat16)
    correction = apply_inverse(newton_residual, inverse_blocks)
    remainder = newton_residual
    for sweep_index in range(ITERS):
        applied = apply_jacobian(correction, coeff_terms, triple_blocks, block_columns, global_ids, tables, embed_matrix)
        remainder = newton_residual - applied
        correction = correction + RELAX_WEIGHT * apply_inverse(remainder, inverse_blocks)
    return (correction, remainder)
```

```python
import functools
import math

import jax
import jax.numpy as jnp
import numpy as np
from jax import lax
from jax.experimental import pallas as pl
from jax.experimental.pallas import tpu as pltpu
from jax.sharding import PartitionSpec as P

K = 84
S = 1024
ITERS = 2
MB = 60
ROWS = 64
NODES = 1024
PAIRS = 42
GROWTH = 0.5
TIME_STEP = 0.03
LIFT_SCALE = 6.0
PENALTY = 3.0
RELAX_WEIGHT = 0.8
FACE_OPPOSITE = (1, 0, 3, 2, 5, 4)
BF = jnp.bfloat16
F32 = jnp.float32
VMEM = pl.BlockSpec(memory_space=pltpu.VMEM)
SMEM = pl.BlockSpec(memory_space=pltpu.SMEM)
ANY = pl.BlockSpec(memory_space=pl.ANY)


def line_derivative():
    inward = 1.0 / math.sqrt(5.0)
    points = np.array([-1.0, -inward, inward, 1.0])
    legendre = (5.0 * points**3 - 3.0 * points) / 2.0
    matrix = np.zeros((4, 4))
    for source in range(4):
        for target in range(4):
            if source != target:
                matrix[source, target] = legendre[source] / (
                    legendre[target] * (points[source] - points[target])
                )
    matrix[0, 0] = -3.0
    matrix[3, 3] = 3.0
    return matrix


def direction_tables():
    line_matrix = line_derivative()
    identity = np.eye(4)
    singles = [
        np.kron(np.kron(line_matrix, identity), identity),
        np.kron(np.kron(identity, line_matrix), identity),
        np.kron(np.kron(identity, identity), line_matrix),
    ]
    return [np.kron(np.eye(2), single).T.astype(np.float32) for single in singles]


def face_nodes():
    layout = np.arange(64).reshape(4, 4, 4)
    return [
        layout[:, 0, :].ravel(),
        layout[:, 3, :].ravel(),
        layout[:, :, 0].ravel(),
        layout[:, :, 3].ravel(),
        layout[0].ravel(),
        layout[3].ravel(),
    ]


def two_parts(table):
    high = np.asarray(table, np.float32).astype(jnp.bfloat16)
    low = (np.asarray(table, np.float32) - high.astype(np.float32)).astype(jnp.bfloat16)
    return high, low


def gradient_table():
    high, low = two_parts(np.concatenate(direction_tables(), axis=1))
    return np.concatenate([high, low], axis=0)


def own_tables():
    tables = direction_tables()
    nodes = face_nodes()
    result = []
    for axis, faces in enumerate(((4, 5), (0, 1), (2, 3))):
        table = tables[axis].copy()
        for sign, face in zip((-1.0, 1.0), faces):
            for node in nodes[face]:
                for half in (0, 64):
                    table[half + node, half + node] -= 0.5 * LIFT_SCALE * sign
        result.append(table)
    high, low = two_parts(np.concatenate(result, axis=0))
    return np.stack([high, low])


def near_table():
    nodes = face_nodes()
    table = np.zeros((256, 128), np.float32)
    for face in range(4):
        for source, target in zip(nodes[FACE_OPPOSITE[face]], nodes[face]):
            table[64 * face + source, target] = 1.0
            table[64 * face + source, 64 + target] = 1.0
    return table.astype(jnp.bfloat16)


def trace_table():
    table = np.zeros((2, 512, 128), np.float32)
    for element in range(8):
        for node in range(16):
            table[0, 64 * element + node, 16 * element + node] = 1.0
            table[1, 64 * element + 48 + node, 16 * element + node] = 1.0
    return table.astype(jnp.bfloat16)


def face_count():
    count = np.zeros((1, 128), np.float32)
    for nodes in face_nodes():
        for node in nodes:
            count[0, node] += 1.0
            count[0, 64 + node] += 1.0
    return count


def dot(left, right):
    return jnp.dot(left, right, preferred_element_type=F32)


def split(value):
    high = value.astype(BF)
    return high, (value - high.astype(F32)).astype(BF)


def call(body, outs, ins, scratch=(), name=None, limit=56 << 20):
    specs = [VMEM if isinstance(o, jax.ShapeDtypeStruct) else o for o in outs]
    return pl.pallas_call(
        body,
        out_shape=tuple(outs),
        in_specs=list(ins),
        out_specs=tuple(specs),
        scratch_shapes=list(scratch),
        name=name,
        compiler_params=pltpu.CompilerParams(vmem_limit_bytes=limit),
    )


def stored_body(x_ref, z_ref, wide, tall):
    wide[...] = jnp.zeros_like(wide)
    x = x_ref[...].astype(F32)
    wide[0:60, 0:1260] = x
    wide[64:124, 0:1259] = x[:, 1:]
    for block in range(10):
        tall[128 * block : 128 * block + 128, :] = wide[:, 128 * block : 128 * block + 128].T
    tall[1280:1344, :] = jnp.zeros((64, 128), F32)
    for pair in range(PAIRS):
        z_ref[pair] = tall[pl.ds(2 * pair, 16, stride=K), :].astype(BF)


def turn_body(where_ref, *refs):
    pieces, eye_ref, tt_ref, held, sem = refs[:16], refs[16], refs[17], refs[18], refs[19]
    copies = [
        pltpu.make_async_copy(piece, held.at[where_ref[index]], sem.at[index])
        for index, piece in enumerate(pieces)
    ]
    for copy in copies:
        copy.start()
    for copy in copies:
        copy.wait()

    def step(pair, carry):
        block = held[:, pair].reshape(256, 128)
        turned = lax.dot_general(
            eye_ref[...], block, (((1,), (1,)), ((), ())), preferred_element_type=F32
        ).astype(BF)
        for half in range(2):
            for tile in range(4):
                first = 64 * half + 16 * tile
                tt_ref[tile, 2 * pair + half] = turned[first : first + 16]
        return carry

    lax.fori_loop(0, PAIRS, step, 0, unroll=6)


def coefficient_body(low_ref, basis_ref, lead_ref, c_ref, joined):
    for block in range(8):
        joined[60 * block : 60 * block + 60, :] = low_ref[block].astype(F32)
    sampled = dot(basis_ref[...], joined[...].astype(BF))
    growth = jnp.exp(GROWTH * sampled)
    high, rest = split(growth)
    middle, low = split(growth - high.astype(F32))
    lead = lead_ref[...]
    c_ref[...] = ((dot(lead, high) + dot(lead, middle) + dot(lead, low)) * (1.0 / S)).astype(BF)


def invert(field, inv_ref, out_ref, base, weight):
    lane = lax.broadcasted_iota(jnp.int32, (64, 128), 1)
    first = lane < 64
    for pair in range(8):
        cols = slice(128 * pair, 128 * pair + 128)
        tile = inv_ref[:, cols]
        block = jnp.concatenate([jnp.where(first, tile, 0.0), jnp.where(first, 0.0, tile)], axis=0)
        high, low = split(block)
        fh, fl = split(field[:, cols])
        value = dot(fh, high) + dot(fl, high) + dot(fh, low)
        out_ref[:, cols] = value if base is None else base[:, cols] + weight * value


def pad_modes(value_ref, padded, wp_ref):
    padded[...] = jnp.zeros_like(padded)
    for group in range(4):
        padded[16 * group : 16 * group + 15, :] = value_ref[15 * group : 15 * group + 15, :]
    wp_ref[...] = padded[...].astype(BF)


def start_body(res_ref, inv_ref, w_ref, wp_ref, field, value, padded):
    field[60:64, :] = jnp.zeros((4, NODES), F32)
    field[0:60, :] = res_ref[...]
    invert(field, inv_ref, value, None, None)
    w_ref[...] = value[0:60, :]
    pad_modes(value, padded, wp_ref)


def flux_body(slot_ref, spot_ref, *refs):
    blocks, coeffs = refs[0:8], refs[8:16]
    tt_ref, table_ref, w_ref, trace_ref = refs[16:20]
    f_ref, toward_ref, onward_ref = refs[20:23]
    picked, cs, cf, grads, sem = refs[23:28]
    for stored in range(4):
        for index in range(8):

            @pl.when(slot_ref[stored] == index)
            def _(stored=stored, index=index):
                pltpu.make_async_copy(blocks[index], picked.at[stored], sem.at[stored]).start()

    copies = [
        pltpu.make_async_copy(coeffs[index], cs.at[spot_ref[index]], sem.at[4 + index])
        for index in range(8)
    ]
    for copy in copies:
        copy.start()
    for stored in range(4):
        pltpu.make_async_copy(blocks[0], picked.at[stored], sem.at[stored]).wait()
    for pair in range(8):
        tile = picked[:, :, 128 * pair : 128 * pair + 128].reshape(256, 128)
        values = dot(jnp.concatenate([tile, tile], axis=1), table_ref[...]).astype(BF)
        for axis in range(3):
            grads[2 * axis + pair // 4, :, 128 * (pair % 4) : 128 * (pair % 4) + 128] = values[
                :, 128 * axis : 128 * axis + 128
            ]
    for copy in copies:
        copy.wait()
    for index in range(8):
        cf[index // 4, :, 128 * (index % 4) : 128 * (index % 4) + 128] = cs[index].astype(F32)

    def step(tile, carry):
        grad = grads[tile]
        half = lax.rem(tile, 2)
        for part in range(4):
            terms = dot(tt_ref[part].reshape(K * 16, 256), grad)
            total = None
            for k in range(K):
                term = cf[half, k : k + 1, :] * terms[16 * k : 16 * k + 16]
                total = term if total is None else total + term
            f_ref[tile, 16 * part : 16 * part + 16, :] = total.astype(BF)
        return carry

    lax.fori_loop(0, 6, step, 0)
    zero = jnp.zeros((4, 512), F32)
    for half in range(2):
        value = (LIFT_SCALE * PENALTY) * jnp.concatenate(
            [w_ref[:, 512 * half : 512 * half + 512], zero], axis=0
        )
        flux = (0.5 * LIFT_SCALE) * f_ref[half].astype(F32)
        for table, mixed, out_ref in (
            (trace_ref[0], value + flux, toward_ref),
            (trace_ref[1], value - flux, onward_ref),
        ):
            high, low = split(mixed)
            out_ref[:, 128 * half : 128 * half + 128] = dot(high, table) + dot(low, table)


def update_body(
    ids_ref, target_ref, w_ref, f_ref, up_ref, un_ref, res_ref, inv_ref, own_ref, near_ref, count_ref,
    rem_ref, corr_ref, wp_ref, v, faces, rem, value, padded,
):
    lane = lax.broadcasted_iota(jnp.int32, (64, 128), 1)
    first = lane < 64
    v[60:64, :] = jnp.zeros((4, NODES), F32)
    v[0:60, :] = w_ref[...]
    rem[60:64, :] = jnp.zeros((4, NODES), F32)
    rem[0:60, :] = res_ref[...]

    def flux(axis, pair):
        return f_ref[2 * axis + pair // 4, :, 128 * (pair % 4) : 128 * (pair % 4) + 128]

    for pair in range(8):
        scaled = (LIFT_SCALE * PENALTY) * v[:, 128 * pair : 128 * pair + 128]
        for axis in (1, 2):
            part = (0.5 * LIFT_SCALE) * flux(axis, pair).astype(F32)
            for side, mixed in enumerate((scaled - part, scaled + part)):
                face = 2 * (axis - 1) + side
                turned = pltpu.roll(mixed, 64, axis=1)
                faces[face, 2 * pair] = jnp.where(first, mixed, turned)
                faces[face, 2 * pair + 1] = jnp.where(first, turned, mixed)
    near = []
    for element in range(16):
        left = jnp.where(first, faces[0, ids_ref[element, 0]], faces[1, ids_ref[element, 1]])
        right = jnp.where(first, faces[2, ids_ref[element, 2]], faces[3, ids_ref[element, 3]])
        high, low = split(jnp.concatenate([left, right], axis=1))
        near.append(dot(high, near_ref[...]) + dot(low, near_ref[...]))
    row = lax.broadcasted_iota(jnp.int32, (256, 128), 0)
    uh, ul = split(up_ref[...])
    nh, nl = split(un_ref[...])
    for pair in range(8):
        cols = slice(128 * pair, 128 * pair + 128)
        lower = jnp.where(row == target_ref[0:1, cols], 1.0, 0.0).astype(BF)
        upper = jnp.where(row == target_ref[1:2, cols], 1.0, 0.0).astype(BF)
        across = dot(uh, lower) + dot(ul, lower) + dot(nh, upper) + dot(nl, upper)
        joined = jnp.concatenate([flux(axis, pair) for axis in range(3)], axis=1)
        inside = dot(joined, own_ref[0]) + dot(joined, own_ref[1])
        here = v[:, cols]
        divergence = (
            inside
            + jnp.where(first, near[2 * pair], near[2 * pair + 1])
            + across
            - (LIFT_SCALE * PENALTY) * count_ref[...] * here
        )
        rem[:, cols] = rem[:, cols] - (here - TIME_STEP * divergence)
    invert(rem, inv_ref, value, v, RELAX_WEIGHT)
    rem_ref[...] = rem[0:60, :]
    corr_ref[...] = value[0:60, :]
    pad_modes(value, padded, wp_ref)


def shaped(shape, dtype):
    return jax.ShapeDtypeStruct(shape, dtype)


def pairs_of(count, move):
    return [(index, move(index)) for index in range(count)]


def over_mode(block):
    def along(step):
        return pairs_of(8, lambda i: ((i // 2 + step) % 4) * 2 + i % 2)

    other = lax.ppermute(block, "mode", pairs_of(8, lambda i: i ^ 1))
    pieces = [block] + [lax.ppermute(block, "mode", along(step)) for step in (1, 2, 3)]
    return pieces + [other] + [lax.ppermute(other, "mode", along(step)) for step in (1, 2, 3)]


def over_elem(block):
    def along(step):
        return pairs_of(16, lambda i: (i & 8) | ((i + 2 * step) & 7))

    far = lax.ppermute(block, "elem", pairs_of(16, lambda i: i ^ 8))
    pieces = [block] + [lax.ppermute(block, "elem", along(step)) for step in (1, 2, 3)]
    pieces += [far] + [lax.ppermute(far, "elem", along(step)) for step in (1, 2, 3)]
    return pieces + [lax.ppermute(piece, "elem", pairs_of(16, lambda i: i ^ 1)) for piece in pieces]


def per_device(
    iterate,
    newton_residual,
    inverse_blocks,
    basis_values,
    triple_blocks,
    block_columns,
    neighbour_ids,
):
    mode = lax.axis_index("mode")
    elem = lax.axis_index("elem")
    steps = jnp.arange(8, dtype=jnp.int32)
    spots = ((mode // 2 - steps % 4) % 4) * 2 + ((mode % 2) ^ (steps // 4))
    columns = block_columns[0]
    slots = (mode // 2 - columns // 2) % 4 + 4 * ((mode % 2) ^ (columns % 2))
    order = jnp.arange(16, dtype=jnp.int32)
    base = (elem & 8) ^ (8 * ((order // 4) % 2))
    places = base | (((elem & 7) - 2 * (order % 4)) & 7)
    places = places ^ (order // 8)
    node = jnp.arange(NODES, dtype=jnp.int32)
    inner = node % 64
    low_ids = jnp.repeat(neighbour_ids[:, 4], 64)
    high_ids = jnp.repeat(neighbour_ids[:, 5], 64)
    targets = jnp.stack(
        [
            jnp.where(inner < 16, 16 * low_ids + inner, -1),
            jnp.where(inner >= 48, 16 * high_ids + inner - 48, -1),
        ]
    )
    mode_rows = shaped((MB, NODES), F32)
    padded_rows = shaped((ROWS, NODES), BF)
    tile = pltpu.VMEM((ROWS, NODES), F32)

    (stored,) = call(
        stored_body,
        (shaped((PAIRS, 16, 128), BF),),
        (VMEM,),
        (pltpu.VMEM((128, 1280), F32), pltpu.VMEM((1344, 128), F32)),
        "stored",
    )(triple_blocks.reshape(MB, 1260))
    stored_pieces = over_elem(stored)

    low_state = iterate.astype(BF).reshape(MB, 8, 128).transpose(1, 0, 2)
    low_state = lax.all_to_all(low_state, "mode", 0, 0)
    lead = jnp.pad(basis_values[:, :K].T, ((0, 12), (0, 0)))
    (terms,) = call(
        coefficient_body,
        (shaped((96, 128), BF),),
        (VMEM,) * 3,
        (pltpu.VMEM((480, 128), F32),),
        "coefficients",
    )(low_state, basis_values, lead)
    coeff_pieces = over_mode(terms)

    correction, padded = call(
        start_body, (mode_rows, padded_rows), (VMEM,) * 2, (tile, tile, tile), "start"
    )(newton_residual, inverse_blocks)

    (turned,) = call(
        turn_body,
        (shaped((4, K, 16, 256), BF),),
        (SMEM,) + (ANY,) * 16 + (VMEM,),
        (pltpu.VMEM((16, PAIRS, 16, 128), BF), pltpu.SemaphoreType.DMA((16,))),
        "turn",
    )(places, *stored_pieces, jnp.asarray(np.eye(128), BF))

    gradients_of = jnp.asarray(gradient_table())
    own = jnp.asarray(own_tables())
    near = jnp.asarray(near_table())
    traces = jnp.asarray(trace_table())
    count = jnp.asarray(face_count())
    remainder = newton_residual
    for sweep in range(ITERS):
        fluxes, toward, onward = call(
            flux_body,
            (shaped((6, ROWS, 512), BF), shaped((ROWS, 256), F32), shaped((ROWS, 256), F32)),
            (SMEM, SMEM) + (ANY,) * 16 + (VMEM,) * 4,
            (
                pltpu.VMEM((4, ROWS, NODES), BF),
                pltpu.VMEM((8, 96, 128), BF),
                pltpu.VMEM((2, 96, 512), F32),
                pltpu.VMEM((6, 256, 512), BF),
                pltpu.SemaphoreType.DMA((12,)),
            ),
            "flux",
        )(slots, spots, *over_mode(padded), *coeff_pieces, turned, gradients_of, correction, traces)
        after = lax.ppermute(toward, "elem", pairs_of(16, lambda i: (i + 15) % 16))
        before = lax.ppermute(onward, "elem", pairs_of(16, lambda i: (i + 1) % 16))
        remainder, correction, padded = call(
            update_body,
            (mode_rows, mode_rows, padded_rows),
            (SMEM,) + (VMEM,) * 10,
            (tile, pltpu.VMEM((4, 16, ROWS, 128), F32), tile, tile, tile),
            "update",
        )(neighbour_ids, targets, correction, fluxes, before, after, newton_residual, inverse_blocks, own, near, count)
    return (correction, remainder)


def solution(mesh):
    return jax.shard_map(
        per_device,
        mesh=mesh,
        in_specs=(
            P("mode", "elem"),
            P("mode", "elem"),
            P(None, "elem"),
            P(),
            P("mode", None, "elem"),
            P("mode", None),
            P("elem", None),
        ),
        out_specs=(P("mode", "elem"), P("mode", "elem")),
        check_vma=False,
    )
```

```python
import math

import jax
import jax.numpy as jnp
import numpy as np
from jax import lax
from jax.experimental import pallas as pl
from jax.experimental.pallas import tpu as pltpu
from jax.sharding import PartitionSpec as P

K = 84
S = 1024
ITERS = 2
MB = 60
ROWS = 64
NODES = 1024
PAIRS = 42
GROWTH = 0.5
TIME_STEP = 0.03
LIFT_SCALE = 6.0
PENALTY = 3.0
RELAX_WEIGHT = 0.8
FACE_OPPOSITE = (1, 0, 3, 2, 5, 4)
BF = jnp.bfloat16
F32 = jnp.float32
VMEM = pl.BlockSpec(memory_space=pltpu.VMEM)
SMEM = pl.BlockSpec(memory_space=pltpu.SMEM)
ANY = pl.BlockSpec(memory_space=pl.ANY)


def line_derivative():
    inward = 1.0 / math.sqrt(5.0)
    points = np.array([-1.0, -inward, inward, 1.0])
    legendre = (5.0 * points**3 - 3.0 * points) / 2.0
    matrix = np.zeros((4, 4))
    for source in range(4):
        for target in range(4):
            if source != target:
                matrix[source, target] = legendre[source] / (
                    legendre[target] * (points[source] - points[target])
                )
    matrix[0, 0] = -3.0
    matrix[3, 3] = 3.0
    return matrix


def direction_tables():
    line_matrix = line_derivative()
    identity = np.eye(4)
    singles = [
        np.kron(np.kron(line_matrix, identity), identity),
        np.kron(np.kron(identity, line_matrix), identity),
        np.kron(np.kron(identity, identity), line_matrix),
    ]
    return [np.kron(np.eye(2), single).T.astype(np.float32) for single in singles]


def face_nodes():
    layout = np.arange(64).reshape(4, 4, 4)
    return [
        layout[:, 0, :].ravel(),
        layout[:, 3, :].ravel(),
        layout[:, :, 0].ravel(),
        layout[:, :, 3].ravel(),
        layout[0].ravel(),
        layout[3].ravel(),
    ]


def two_parts(table):
    high = np.asarray(table, np.float32).astype(jnp.bfloat16)
    low = (np.asarray(table, np.float32) - high.astype(np.float32)).astype(jnp.bfloat16)
    return high, low


def gradient_table():
    high, low = two_parts(np.concatenate(direction_tables(), axis=1))
    return np.concatenate([high, low], axis=0)


def own_tables():
    tables = direction_tables()
    nodes = face_nodes()
    result = []
    for axis, faces in enumerate(((4, 5), (0, 1), (2, 3))):
        table = tables[axis].copy()
        for sign, face in zip((-1.0, 1.0), faces):
            for node in nodes[face]:
                for half in (0, 64):
                    table[half + node, half + node] -= 0.5 * LIFT_SCALE * sign
        result.append(table)
    high, low = two_parts(np.concatenate(result, axis=0))
    return np.stack([high, low])


def near_table():
    nodes = face_nodes()
    table = np.zeros((256, 128), np.float32)
    for face in range(4):
        for source, target in zip(nodes[FACE_OPPOSITE[face]], nodes[face]):
            table[64 * face + source, target] = 1.0
            table[64 * face + source, 64 + target] = 1.0
    return table.astype(jnp.bfloat16)


def trace_table():
    table = np.zeros((2, 512, 128), np.float32)
    for element in range(8):
        for node in range(16):
            table[0, 64 * element + node, 16 * element + node] = 1.0
            table[1, 64 * element + 48 + node, 16 * element + node] = 1.0
    return table.astype(jnp.bfloat16)


def face_count():
    count = np.zeros((1, 128), np.float32)
    for nodes in face_nodes():
        for node in nodes:
            count[0, node] += 1.0
            count[0, 64 + node] += 1.0
    return count


def dot(left, right):
    return jnp.dot(left, right, preferred_element_type=F32)


def split(value):
    high = value.astype(BF)
    return high, (value - high.astype(F32)).astype(BF)


def call(body, outs, ins, scratch=(), limit=56 << 20):
    specs = [VMEM if isinstance(o, jax.ShapeDtypeStruct) else o for o in outs]
    return pl.pallas_call(
        body,
        out_shape=tuple(outs),
        in_specs=list(ins),
        out_specs=tuple(specs),
        scratch_shapes=list(scratch),
        compiler_params=pltpu.CompilerParams(vmem_limit_bytes=limit),
    )


def stored_body(x_ref, z_ref, wide, tall):
    wide[...] = jnp.zeros_like(wide)
    x = x_ref[...].astype(F32)
    wide[0:60, 0:1260] = x
    wide[64:124, 0:1259] = x[:, 1:]
    for block in range(10):
        tall[128 * block : 128 * block + 128, :] = wide[:, 128 * block : 128 * block + 128].T
    tall[1280:1344, :] = jnp.zeros((64, 128), F32)
    for pair in range(PAIRS):
        z_ref[pair] = tall[pl.ds(2 * pair, 16, stride=K), :].astype(BF)


def turn_body(side_ref, held, eye_ref, tt_ref):
    side = side_ref[0]

    def step(twin, carry):
        rows = []
        for place in range(8):
            zone = side if place < 4 else 1 - side
            rows.append(held[place % 4, zone, pl.ds(2 * twin, 2)])
        both = jnp.concatenate([row[pair] for pair in range(2) for row in rows], axis=0)
        turned = lax.dot_general(
            eye_ref[...], both, (((1,), (1,)), ((), ())), preferred_element_type=F32
        ).astype(BF)
        for pair in range(2):
            for half in range(2):
                for tile in range(4):
                    first = 64 * half + 16 * tile
                    tt_ref[tile, 4 * twin + 2 * pair + half] = turned[
                        first : first + 16, 128 * pair : 128 * pair + 128
                    ]
        return carry

    lax.fori_loop(0, PAIRS // 2, step, 0, unroll=3)


def coefficient_body(spot_ref, *refs):
    pieces, basis_ref, lead_ref, c_ref, low, sem = refs[:8], refs[8], refs[9], refs[10], refs[11], refs[12]
    copies = [
        pltpu.make_async_copy(piece.at[64:128], low.at[spot_ref[index]], sem.at[index])
        for index, piece in enumerate(pieces)
    ]
    for copy in copies:
        copy.start()
    for copy in copies:
        copy.wait()
    lead = lead_ref[...]
    for quarter in range(4):
        state = low[:, :, 256 * quarter : 256 * quarter + 256].reshape(512, 256)
        growth = jnp.exp(GROWTH * dot(basis_ref[...], state))
        high, rest = split(growth)
        terms = (dot(lead, high) + dot(lead, rest)) * (1.0 / S)
        c_ref[quarter // 2, :, 256 * (quarter % 2) : 256 * (quarter % 2) + 256] = terms.astype(BF).astype(F32)


def invert(field, inv_ref, out_ref, base, weight):
    lane = lax.broadcasted_iota(jnp.int32, (64, 128), 1)
    first = lane < 64
    for pair in range(8):
        cols = slice(128 * pair, 128 * pair + 128)
        tile = inv_ref[:, cols]
        block = jnp.concatenate([jnp.where(first, tile, 0.0), jnp.where(first, 0.0, tile)], axis=0)
        high, low = split(block)
        fh, fl = split(field[:, cols])
        value = dot(fh, high) + dot(fl, high) + dot(fh, low)
        out_ref[:, cols] = value if base is None else base[:, cols] + weight * value


def pad_modes(value_ref, padded, wp_ref):
    padded[...] = jnp.zeros_like(padded)
    for group in range(4):
        padded[16 * group : 16 * group + 15, :] = value_ref[15 * group : 15 * group + 15, :]
    wp_ref[0:64, :] = padded[...].astype(BF)


def start_body(res_ref, inv_ref, state_ref, w_ref, wp_ref, field, value, padded):
    field[60:64, :] = jnp.zeros((4, NODES), F32)
    field[0:60, :] = state_ref[...]
    wp_ref[64:128, :] = field[...].astype(BF)
    field[60:64, :] = jnp.zeros((4, NODES), F32)
    field[0:60, :] = res_ref[...]
    invert(field, inv_ref, value, None, None)
    w_ref[...] = value[0:60, :]
    pad_modes(value, padded, wp_ref)


def weighted(mine_ref, theirs_ref, grad, cf, half, out_ref, tile):
    for part in range(4):
        left = jnp.concatenate(
            [mine_ref[part].reshape(K * 16, 128), theirs_ref[part].reshape(K * 16, 128)], axis=1
        )
        terms = dot(left, grad)
        total = None
        for k in range(K):
            term = cf[half, k : k + 1, :] * terms[16 * k : 16 * k + 16]
            total = term if total is None else total + term
        out_ref[tile, 16 * part : 16 * part + 16, :] = total.astype(BF)


def along_body(slot_ref, core_ref, *refs):
    blocks = refs[0:8]
    mine_ref, theirs_ref, cf, table_ref, w_ref, trace_ref = refs[8:14]
    f_ref, toward_ref, onward_ref, grads_ref = refs[14:18]
    picked, first_grads, sem = refs[18:21]
    for stored in range(4):
        for index in range(8):

            @pl.when(slot_ref[stored] == index)
            def _(stored=stored, index=index):
                pltpu.make_async_copy(
                    blocks[index].at[0:64], picked.at[stored], sem.at[stored]
                ).start()

    for stored in range(4):
        pltpu.make_async_copy(blocks[0].at[0:64], picked.at[stored], sem.at[stored]).wait()
    core = core_ref[0]
    for pair in range(8):
        tile = picked[:, :, 128 * pair : 128 * pair + 128].reshape(256, 128)
        values = dot(jnp.concatenate([tile, tile], axis=1), table_ref[...]).astype(BF)
        cols = slice(128 * (pair % 4), 128 * (pair % 4) + 128)
        for source in range(16):
            spot = (source // 2) + 8 * (core if source % 2 == 0 else 1 - core)
            for axis in range(3):
                rows = values[16 * source : 16 * source + 16, 128 * axis : 128 * axis + 128]
                if axis == 0:
                    first_grads[pair // 4, spot, :, cols] = rows
                else:
                    grads_ref[2 * (axis - 1) + pair // 4, spot, :, cols] = rows

    def step(half, carry):
        grad = first_grads[half].reshape(256, 512)
        weighted(mine_ref, theirs_ref, grad, cf, half, f_ref, half)
        return carry

    lax.fori_loop(0, 2, step, 0)
    zero = jnp.zeros((4, 512), F32)
    for half in range(2):
        value = (LIFT_SCALE * PENALTY) * jnp.concatenate(
            [w_ref[:, 512 * half : 512 * half + 512], zero], axis=0
        )
        flux = (0.5 * LIFT_SCALE) * f_ref[half].astype(F32)
        for table, mixed, out_ref in (
            (trace_ref[0], value + flux, toward_ref),
            (trace_ref[1], value - flux, onward_ref),
        ):
            high, low = split(mixed)
            out_ref[:, 128 * half : 128 * half + 128] = dot(high, table) + dot(low, table)


def across_body(mine_ref, theirs_ref, cf, grads_ref, f_ref):
    def step(tile, carry):
        grad = grads_ref[tile].reshape(256, 512)
        weighted(mine_ref, theirs_ref, grad, cf, lax.rem(tile, 2), f_ref, tile)
        return carry

    lax.fori_loop(0, 4, step, 0)


def update_body(
    ids_ref, w_ref, fx_ref, f_ref, up_ref, un_ref, res_ref, inv_ref, own_ref, near_ref, count_ref,
    rem_ref, corr_ref, wp_ref, v, faces, rem, value, padded,
):
    lane = lax.broadcasted_iota(jnp.int32, (64, 128), 1)
    first = lane < 64
    v[60:64, :] = jnp.zeros((4, NODES), F32)
    v[0:60, :] = w_ref[...]
    rem[60:64, :] = jnp.zeros((4, NODES), F32)
    rem[0:60, :] = res_ref[...]

    def flux(axis, pair):
        source, index = (fx_ref, pair // 4) if axis == 0 else (f_ref, 2 * (axis - 1) + pair // 4)
        return source[index, :, 128 * (pair % 4) : 128 * (pair % 4) + 128]

    for pair in range(8):
        scaled = (LIFT_SCALE * PENALTY) * v[:, 128 * pair : 128 * pair + 128]
        for axis in (1, 2):
            part = (0.5 * LIFT_SCALE) * flux(axis, pair).astype(F32)
            for side, mixed in enumerate((scaled - part, scaled + part)):
                face = 2 * (axis - 1) + side
                turned = pltpu.roll(mixed, 64, axis=1)
                faces[face, 2 * pair] = jnp.where(first, mixed, turned)
                faces[face, 2 * pair + 1] = jnp.where(first, turned, mixed)
    near = []
    for element in range(16):
        left = jnp.where(first, faces[0, ids_ref[element, 0]], faces[1, ids_ref[element, 1]])
        right = jnp.where(first, faces[2, ids_ref[element, 2]], faces[3, ids_ref[element, 3]])
        high, low = split(jnp.concatenate([left, right], axis=1))
        near.append(dot(high, near_ref[...]) + dot(low, near_ref[...]))
    row = lax.broadcasted_iota(jnp.int32, (256, 128), 0)
    column = lax.broadcasted_iota(jnp.int32, (1, 128), 1)
    inner = column % 64
    uh, ul = split(up_ref[...])
    nh, nl = split(un_ref[...])
    for pair in range(8):
        cols = slice(128 * pair, 128 * pair + 128)
        left, right = 2 * pair, 2 * pair + 1
        below = 16 * jnp.where(column < 64, ids_ref[left, 4], ids_ref[right, 4]) + inner
        above = 16 * jnp.where(column < 64, ids_ref[left, 5], ids_ref[right, 5]) + inner - 48
        lower = jnp.where(row == jnp.where(inner < 16, below, -1), 1.0, 0.0).astype(BF)
        upper = jnp.where(row == jnp.where(inner >= 48, above, -1), 1.0, 0.0).astype(BF)
        across = dot(uh, lower) + dot(ul, lower) + dot(nh, upper) + dot(nl, upper)
        joined = jnp.concatenate([flux(axis, pair) for axis in range(3)], axis=1)
        inside = dot(joined, own_ref[0]) + dot(joined, own_ref[1])
        here = v[:, cols]
        divergence = (
            inside
            + jnp.where(first, near[2 * pair], near[2 * pair + 1])
            + across
            - (LIFT_SCALE * PENALTY) * count_ref[...] * here
        )
        rem[:, cols] = rem[:, cols] - (here - TIME_STEP * divergence)
    invert(rem, inv_ref, value, v, RELAX_WEIGHT)
    rem_ref[...] = rem[0:60, :]
    corr_ref[...] = value[0:60, :]
    pad_modes(value, padded, wp_ref)


def shaped(shape, dtype):
    return jax.ShapeDtypeStruct(shape, dtype)


def pairs_of(count, move):
    return [(index, move(index)) for index in range(count)]


def over_mode(block):
    def along(step):
        return pairs_of(8, lambda i: ((i // 2 + step) % 4) * 2 + i % 2)

    flip = pairs_of(8, lambda i: i ^ 1)
    other = lax.ppermute(block, "mode", flip)
    one = lax.ppermute(block, "mode", along(1))
    two = lax.ppermute(block, "mode", along(2))
    three = lax.ppermute(block, "mode", along(3))
    return [
        block,
        one,
        two,
        three,
        other,
        lax.ppermute(other, "mode", along(1)),
        lax.ppermute(two, "mode", flip),
        lax.ppermute(other, "mode", along(3)),
    ]


def per_device(
    iterate,
    newton_residual,
    inverse_blocks,
    basis_values,
    triple_blocks,
    block_columns,
    neighbour_ids,
):
    mode = lax.axis_index("mode")
    elem = lax.axis_index("elem")
    steps = jnp.arange(8, dtype=jnp.int32)
    spots = ((mode // 2 - steps % 4) % 4) * 2 + ((mode % 2) ^ (steps // 4))
    columns = block_columns[0]
    slots = (mode // 2 - columns // 2) % 4 + 4 * ((mode % 2) ^ (columns % 2))
    core = (elem & 1)[None]
    side = (elem // 8)[None]
    mode_rows = shaped((MB, NODES), F32)
    padded_rows = shaped((ROWS, NODES), BF)
    tile = pltpu.VMEM((ROWS, NODES), F32)

    (stored,) = call(
        stored_body,
        (shaped((PAIRS, 16, 128), BF),),
        (VMEM,),
        (pltpu.VMEM((128, 1280), F32), pltpu.VMEM((1344, 128), F32)),
    )(triple_blocks.reshape(MB, 1260))
    far = lax.ppermute(stored, "elem", pairs_of(16, lambda i: i ^ 8))
    groups = [[8 * zone + 2 * y + c for y in range(4)] for zone in range(2) for c in range(2)]
    sent = jnp.broadcast_to(jnp.stack([stored, far]), (4, 2, PAIRS, 16, 128))
    held = lax.all_to_all(sent, "elem", 0, 0, axis_index_groups=groups)
    correction, padded = call(
        start_body, (mode_rows, shaped((128, NODES), BF)), (VMEM,) * 3, (tile, tile, tile)
    )(newton_residual, inverse_blocks, iterate)
    pieces = over_mode(padded)

    lead = jnp.pad(basis_values[:, :K].T, ((0, 12), (0, 0)))
    spread = jnp.pad(basis_values.reshape(S, 8, MB), ((0, 0), (0, 0), (0, 4))).reshape(S, 512)
    held, spread, lead, slots, spots, ids = lax.optimization_barrier(
        (held, spread, lead, slots, spots, neighbour_ids)
    )
    (mine,) = call(turn_body, (shaped((4, K, 16, 128), BF),), (SMEM,) + (VMEM,) * 2, ())(
        side, held, jnp.asarray(np.eye(128), BF)
    )
    theirs = lax.ppermute(mine, "elem", pairs_of(16, lambda i: i ^ 1))
    (coeffs,) = call(
        coefficient_body,
        (shaped((2, 96, 512), F32),),
        (SMEM,) + (ANY,) * 8 + (VMEM,) * 2,
        (pltpu.VMEM((8, 64, NODES), BF), pltpu.SemaphoreType.DMA((8,))),
    )(spots, *pieces, spread, lead)


    gradients_of = jnp.asarray(gradient_table())
    own = jnp.asarray(own_tables())
    near = jnp.asarray(near_table())
    traces = jnp.asarray(trace_table())
    count = jnp.asarray(face_count())
    remainder = newton_residual
    for sweep in range(ITERS):
        along, toward, onward, grads = call(
            along_body,
            (
                shaped((2, ROWS, 512), BF),
                shaped((ROWS, 256), F32),
                shaped((ROWS, 256), F32),
                shaped((4, 16, 16, 512), BF),
            ),
            (SMEM, SMEM) + (ANY,) * 8 + (VMEM,) * 6,
            (
                pltpu.VMEM((4, ROWS, NODES), BF),
                pltpu.VMEM((2, 16, 16, 512), BF),
                pltpu.SemaphoreType.DMA((4,)),
            ),
        )(slots, core, *pieces, mine, theirs, coeffs, gradients_of, correction, traces)
        after = lax.ppermute(toward, "elem", pairs_of(16, lambda i: (i + 15) % 16))
        before = lax.ppermute(onward, "elem", pairs_of(16, lambda i: (i + 1) % 16))
        (across,) = call(across_body, (shaped((4, ROWS, 512), BF),), (VMEM,) * 4, ())(
            mine, theirs, coeffs, grads
        )
        remainder, correction, padded = call(
            update_body,
            (mode_rows, mode_rows, padded_rows),
            (SMEM,) + (VMEM,) * 10,
            (tile, pltpu.VMEM((4, 16, ROWS, 128), F32), tile, tile, tile),
        )(ids, correction, along, across, before, after, newton_residual, inverse_blocks, own, near, count)
        pieces = over_mode(padded) if sweep + 1 < ITERS else None
    return (correction, remainder)


def solution(mesh):
    return jax.shard_map(
        per_device,
        mesh=mesh,
        in_specs=(
            P("mode", "elem"),
            P("mode", "elem"),
            P(None, "elem"),
            P(),
            P("mode", None, "elem"),
            P("mode", None),
            P("elem", None),
        ),
        out_specs=(P("mode", "elem"), P("mode", "elem")),
        check_vma=False,
    )
```

```python
import math

import jax
import jax.numpy as jnp
import numpy as np
from jax import lax
from jax.experimental import pallas as pl
from jax.experimental.pallas import tpu as pltpu
from jax.sharding import PartitionSpec as P

K = 84
S = 1024
ITERS = 2
MB = 60
ROWS = 64
NODES = 1024
PAIRS = 42
GROWTH = 0.5
TIME_STEP = 0.03
LIFT_SCALE = 6.0
PENALTY = 3.0
RELAX_WEIGHT = 0.8
FACE_OPPOSITE = (1, 0, 3, 2, 5, 4)
BF = jnp.bfloat16
F32 = jnp.float32
VMEM = pl.BlockSpec(memory_space=pltpu.VMEM)
SMEM = pl.BlockSpec(memory_space=pltpu.SMEM)
ANY = pl.BlockSpec(memory_space=pl.ANY)
FAR = pl.BlockSpec(memory_space=pltpu.HBM)


def line_derivative():
    inward = 1.0 / math.sqrt(5.0)
    points = np.array([-1.0, -inward, inward, 1.0])
    legendre = (5.0 * points**3 - 3.0 * points) / 2.0
    matrix = np.zeros((4, 4))
    for source in range(4):
        for target in range(4):
            if source != target:
                matrix[source, target] = legendre[source] / (
                    legendre[target] * (points[source] - points[target])
                )
    matrix[0, 0] = -3.0
    matrix[3, 3] = 3.0
    return matrix


def direction_tables():
    line_matrix = line_derivative()
    identity = np.eye(4)
    singles = [
        np.kron(np.kron(line_matrix, identity), identity),
        np.kron(np.kron(identity, line_matrix), identity),
        np.kron(np.kron(identity, identity), line_matrix),
    ]
    return [np.kron(np.eye(2), single).T.astype(np.float32) for single in singles]


def face_nodes():
    layout = np.arange(64).reshape(4, 4, 4)
    return [
        layout[:, 0, :].ravel(),
        layout[:, 3, :].ravel(),
        layout[:, :, 0].ravel(),
        layout[:, :, 3].ravel(),
        layout[0].ravel(),
        layout[3].ravel(),
    ]


def two_parts(table):
    high = np.asarray(table, np.float32).astype(jnp.bfloat16)
    low = (np.asarray(table, np.float32) - high.astype(np.float32)).astype(jnp.bfloat16)
    return high, low


def gradient_table():
    high, low = two_parts(np.concatenate(direction_tables(), axis=1))
    return np.concatenate([high, low], axis=0)


def own_tables():
    tables = direction_tables()
    nodes = face_nodes()
    result = []
    for axis, faces in enumerate(((4, 5), (0, 1), (2, 3))):
        table = tables[axis].copy()
        for sign, face in zip((-1.0, 1.0), faces):
            for node in nodes[face]:
                for half in (0, 64):
                    table[half + node, half + node] -= 0.5 * LIFT_SCALE * sign
        result.append(table)
    high, low = two_parts(np.concatenate(result, axis=0))
    return np.stack([high, low])


def near_table():
    nodes = face_nodes()
    table = np.zeros((256, 128), np.float32)
    for face in range(4):
        for source, target in zip(nodes[FACE_OPPOSITE[face]], nodes[face]):
            table[64 * face + source, target] = 1.0
            table[64 * face + source, 64 + target] = 1.0
    return table.astype(jnp.bfloat16)


def trace_table():
    table = np.zeros((2, 512, 128), np.float32)
    for element in range(8):
        for node in range(16):
            table[0, 64 * element + node, 16 * element + node] = 1.0
            table[1, 64 * element + 48 + node, 16 * element + node] = 1.0
    return table.astype(jnp.bfloat16)


def face_count():
    count = np.zeros((1, 128), np.float32)
    for nodes in face_nodes():
        for node in nodes:
            count[0, node] += 1.0
            count[0, 64 + node] += 1.0
    return count


def dot(left, right):
    return jnp.dot(left, right, preferred_element_type=F32)


def split(value):
    high = value.astype(BF)
    return high, (value - high.astype(F32)).astype(BF)


def call(body, outs, ins, scratch=(), limit=20 << 20):
    specs = [VMEM if isinstance(o, jax.ShapeDtypeStruct) else o for o in outs]
    return pl.pallas_call(
        body,
        out_shape=tuple(outs),
        in_specs=list(ins),
        out_specs=tuple(specs),
        scratch_shapes=list(scratch),
        compiler_params=pltpu.CompilerParams(vmem_limit_bytes=limit),
    )


def fetch(sources, targets, sem):
    copies = [
        pltpu.make_async_copy(source, target, sem.at[index])
        for index, (source, target) in enumerate(zip(sources, targets))
    ]
    for copy in copies:
        copy.start()
    return copies


def stored_body(x_ref, z_ref, wide, tall):
    wide[...] = jnp.zeros_like(wide)
    x = x_ref[...].astype(F32)
    wide[0:60, 0:1260] = x
    wide[64:124, 0:1259] = x[:, 1:]
    for block in range(10):
        tall[128 * block : 128 * block + 128, :] = wide[:, 128 * block : 128 * block + 128].T
    tall[1280:1344, :] = jnp.zeros((64, 128), F32)
    for pair in range(PAIRS):
        z_ref[pair] = tall[pl.ds(2 * pair, 16, stride=K), :].astype(BF)


def turn_body(side_ref, ids_ref, held, eye_ref, tt_ref):
    side = side_ref[0]

    def step(twin, carry):
        rows = []
        for place in range(8):
            zone = side if place < 4 else 1 - side
            rows.append(held[place % 4, zone, pl.ds(2 * twin, 2)])
        both = jnp.concatenate([row[pair] for pair in range(2) for row in rows], axis=0)
        turned = lax.dot_general(
            eye_ref[...], both, (((1,), (1,)), ((), ())), preferred_element_type=F32
        ).astype(BF)
        for pair in range(2):
            for half in range(2):
                for tile in range(4):
                    first = 64 * half + 16 * tile
                    tt_ref[tile, 4 * twin + 2 * pair + half] = turned[
                        first : first + 16, 128 * pair : 128 * pair + 128
                    ]
        return carry

    lax.fori_loop(0, PAIRS // 2, step, 0, unroll=3)


def coefficient_body(spot_ref, *refs):
    pieces, turned_ref, c_ref = refs[:8], refs[8], refs[9]
    low, joined, turned, basis, sem = refs[10:15]
    copies = fetch(
        [piece.at[64:128] for piece in pieces] + [turned_ref],
        [low.at[spot_ref[index]] for index in range(8)] + [turned],
        sem,
    )
    copies[8].wait()
    for block in range(8):
        rows = turned[:, 128 * block : 128 * block + 128].astype(F32).T
        basis[128 * block : 128 * block + 128, :] = rows.astype(BF)
    lead = turned[0:96, :]
    for copy in copies[:8]:
        copy.wait()
    for block in range(8):
        joined[60 * block : 60 * block + 60, :] = low[block].astype(F32)[0:60]
    for quarter in range(4):
        state = joined[:, 256 * quarter : 256 * quarter + 256].astype(BF)
        growth = jnp.exp(GROWTH * dot(basis[...], state))
        high, rest = split(growth)
        terms = (dot(lead, high) + dot(lead, rest)) * (1.0 / S)
        c_ref[quarter // 2, :, 256 * (quarter % 2) : 256 * (quarter % 2) + 256] = terms.astype(BF).astype(F32)


def invert(field, inv_ref, out_ref, base, weight):
    lane = lax.broadcasted_iota(jnp.int32, (64, 128), 1)
    first = lane < 64
    for pair in range(8):
        cols = slice(128 * pair, 128 * pair + 128)
        tile = inv_ref[:, cols]
        block = jnp.concatenate([jnp.where(first, tile, 0.0), jnp.where(first, 0.0, tile)], axis=0)
        high, low = split(block)
        fh, fl = split(field[:, cols])
        value = dot(fh, high) + dot(fl, high) + dot(fh, low)
        out_ref[:, cols] = value if base is None else base[:, cols] + weight * value


def pad_modes(value_ref, padded, wp_ref):
    padded[...] = jnp.zeros_like(padded)
    for group in range(4):
        padded[16 * group : 16 * group + 15, :] = value_ref[15 * group : 15 * group + 15, :]
    wp_ref[0:64, :] = padded[...].astype(BF)


def start_body(
    res_ref, inv_ref, state_ref, w_ref, wp_ref, field, value, padded, res, inverse, state, sem
):
    copies = fetch((state_ref, res_ref, inv_ref), (state, res, inverse), sem)
    field[60:64, :] = jnp.zeros((4, NODES), F32)
    copies[0].wait()
    field[0:60, :] = state[...]
    wp_ref[64:128, :] = field[...].astype(BF)
    copies[1].wait()
    field[0:60, :] = res[...]
    copies[2].wait()
    invert(field, inverse, value, None, None)
    w_ref[...] = value[0:60, :]
    pad_modes(value, padded, wp_ref)


def weighted(mine_ref, theirs_ref, grad, cf, half, out_ref, tile):
    for part in range(4):
        left = jnp.concatenate(
            [mine_ref[part].reshape(K * 16, 128), theirs_ref[part].reshape(K * 16, 128)], axis=1
        )
        terms = dot(left, grad)
        total = None
        for k in range(K):
            term = cf[half, k : k + 1, :] * terms[16 * k : 16 * k + 16]
            total = term if total is None else total + term
        out_ref[tile, 16 * part : 16 * part + 16, :] = total.astype(BF)


def along_body(slot_ref, core_ref, *refs):
    blocks = refs[0:8]
    mine_ref, theirs_ref, cf, table_src, w_src, trace_src = refs[8:14]
    f_ref, toward_ref, onward_ref, grads_ref = refs[14:18]
    picked, first_grads, sem, table_ref, w_ref, trace_ref, late = refs[18:25]
    copies = fetch((table_src, w_src, trace_src), (table_ref, w_ref, trace_ref), late)
    for stored in range(4):
        for index in range(8):

            @pl.when(slot_ref[stored] == index)
            def _(stored=stored, index=index):
                pltpu.make_async_copy(
                    blocks[index].at[0:64], picked.at[stored], sem.at[stored]
                ).start()

    for stored in range(4):
        pltpu.make_async_copy(blocks[0].at[0:64], picked.at[stored], sem.at[stored]).wait()
    core = core_ref[0]
    copies[0].wait()
    for pair in range(8):
        tile = picked[:, :, 128 * pair : 128 * pair + 128].reshape(256, 128)
        values = dot(jnp.concatenate([tile, tile], axis=1), table_ref[...]).astype(BF)
        cols = slice(128 * (pair % 4), 128 * (pair % 4) + 128)
        for source in range(16):
            spot = (source // 2) + 8 * (core if source % 2 == 0 else 1 - core)
            for axis in range(3):
                rows = values[16 * source : 16 * source + 16, 128 * axis : 128 * axis + 128]
                if axis == 0:
                    first_grads[pair // 4, spot, :, cols] = rows
                else:
                    grads_ref[2 * (axis - 1) + pair // 4, spot, :, cols] = rows

    def step(half, carry):
        grad = first_grads[half].reshape(256, 512)
        weighted(mine_ref, theirs_ref, grad, cf, half, f_ref, half)
        return carry

    lax.fori_loop(0, 2, step, 0)
    copies[1].wait()
    copies[2].wait()
    zero = jnp.zeros((4, 512), F32)
    for half in range(2):
        value = (LIFT_SCALE * PENALTY) * jnp.concatenate(
            [w_ref[:, 512 * half : 512 * half + 512], zero], axis=0
        )
        flux = (0.5 * LIFT_SCALE) * f_ref[half].astype(F32)
        for table, mixed, out_ref in (
            (trace_ref[0], value + flux, toward_ref),
            (trace_ref[1], value - flux, onward_ref),
        ):
            high, low = split(mixed)
            out_ref[:, 128 * half : 128 * half + 128] = dot(high, table) + dot(low, table)


def across_body(mine_ref, theirs_ref, cf, grads_ref, f_ref):
    def step(tile, carry):
        grad = grads_ref[tile].reshape(256, 512)
        weighted(mine_ref, theirs_ref, grad, cf, lax.rem(tile, 2), f_ref, tile)
        return carry

    lax.fori_loop(0, 4, step, 0)


def update_body(
    ids_ref, w_ref, fx_ref, f_ref, up_ref, un_ref, res_ref, inv_ref, own_ref, near_ref, count_ref,
    rem_ref, corr_ref, wp_ref, v, faces, rem, value, padded,
):
    lane = lax.broadcasted_iota(jnp.int32, (64, 128), 1)
    first = lane < 64
    v[60:64, :] = jnp.zeros((4, NODES), F32)
    v[0:60, :] = w_ref[...]
    rem[60:64, :] = jnp.zeros((4, NODES), F32)
    rem[0:60, :] = res_ref[...]

    def flux(axis, pair):
        source, index = (fx_ref, pair // 4) if axis == 0 else (f_ref, 2 * (axis - 1) + pair // 4)
        return source[index, :, 128 * (pair % 4) : 128 * (pair % 4) + 128]

    for pair in range(8):
        scaled = (LIFT_SCALE * PENALTY) * v[:, 128 * pair : 128 * pair + 128]
        for axis in (1, 2):
            part = (0.5 * LIFT_SCALE) * flux(axis, pair).astype(F32)
            for side, mixed in enumerate((scaled - part, scaled + part)):
                face = 2 * (axis - 1) + side
                turned = pltpu.roll(mixed, 64, axis=1)
                faces[face, 2 * pair] = jnp.where(first, mixed, turned)
                faces[face, 2 * pair + 1] = jnp.where(first, turned, mixed)
    near = []
    for element in range(16):
        left = jnp.where(first, faces[0, ids_ref[0, element]], faces[1, ids_ref[1, element]])
        right = jnp.where(first, faces[2, ids_ref[2, element]], faces[3, ids_ref[3, element]])
        high, low = split(jnp.concatenate([left, right], axis=1))
        near.append(dot(high, near_ref[...]) + dot(low, near_ref[...]))
    row = lax.broadcasted_iota(jnp.int32, (256, 128), 0)
    column = lax.broadcasted_iota(jnp.int32, (1, 128), 1)
    inner = column % 64
    uh, ul = split(up_ref[...])
    nh, nl = split(un_ref[...])
    for pair in range(8):
        cols = slice(128 * pair, 128 * pair + 128)
        left, right = 2 * pair, 2 * pair + 1
        below = 16 * jnp.where(column < 64, ids_ref[4, left], ids_ref[4, right]) + inner
        above = 16 * jnp.where(column < 64, ids_ref[5, left], ids_ref[5, right]) + inner - 48
        lower = jnp.where(row == jnp.where(inner < 16, below, -1), 1.0, 0.0).astype(BF)
        upper = jnp.where(row == jnp.where(inner >= 48, above, -1), 1.0, 0.0).astype(BF)
        across = dot(uh, lower) + dot(ul, lower) + dot(nh, upper) + dot(nl, upper)
        joined = jnp.concatenate([flux(axis, pair) for axis in range(3)], axis=1)
        inside = dot(joined, own_ref[0]) + dot(joined, own_ref[1])
        here = v[:, cols]
        divergence = (
            inside
            + jnp.where(first, near[2 * pair], near[2 * pair + 1])
            + across
            - (LIFT_SCALE * PENALTY) * count_ref[...] * here
        )
        rem[:, cols] = rem[:, cols] - (here - TIME_STEP * divergence)
    invert(rem, inv_ref, value, v, RELAX_WEIGHT)
    rem_ref[...] = rem[0:60, :]
    corr_ref[...] = value[0:60, :]
    pad_modes(value, padded, wp_ref)


def shaped(shape, dtype):
    return jax.ShapeDtypeStruct(shape, dtype)


def pairs_of(count, move):
    return [(index, move(index)) for index in range(count)]


def over_mode(block):
    def along(step):
        return pairs_of(8, lambda i: ((i // 2 + step) % 4) * 2 + i % 2)

    flip = pairs_of(8, lambda i: i ^ 1)
    other = lax.ppermute(block, "mode", flip)
    one = lax.ppermute(block, "mode", along(1))
    two = lax.ppermute(block, "mode", along(2))
    three = lax.ppermute(block, "mode", along(3))
    return [
        block,
        one,
        two,
        three,
        other,
        lax.ppermute(other, "mode", along(1)),
        lax.ppermute(two, "mode", flip),
        lax.ppermute(other, "mode", along(3)),
    ]


def per_device(
    iterate,
    newton_residual,
    inverse_blocks,
    basis_values,
    triple_blocks,
    block_columns,
    neighbour_ids,
):
    mode = lax.axis_index("mode")
    elem = lax.axis_index("elem")
    steps = jnp.arange(8, dtype=jnp.int32)
    spots = ((mode // 2 - steps % 4) % 4) * 2 + ((mode % 2) ^ (steps // 4))
    columns = block_columns[0]
    slots = (mode // 2 - columns // 2) % 4 + 4 * ((mode % 2) ^ (columns % 2))
    core = (elem & 1)[None]
    side = (elem // 8)[None]
    mode_rows = shaped((MB, NODES), F32)
    padded_rows = shaped((ROWS, NODES), BF)
    tile = pltpu.VMEM((ROWS, NODES), F32)
    rows = pltpu.VMEM((MB, NODES), F32)

    (stored,) = call(
        stored_body,
        (shaped((PAIRS, 16, 128), BF),),
        (VMEM,),
        (pltpu.VMEM((128, 1280), F32), pltpu.VMEM((1344, 128), F32)),
    )(triple_blocks.reshape(MB, 1260))
    far = lax.ppermute(stored, "elem", pairs_of(16, lambda i: i ^ 8))
    groups = [[8 * zone + 2 * y + c for y in range(4)] for zone in range(2) for c in range(2)]
    sent = jnp.broadcast_to(jnp.stack([stored, far]), (4, 2, PAIRS, 16, 128))
    held = lax.all_to_all(sent, "elem", 0, 0, axis_index_groups=groups)
    correction, padded = call(
        start_body,
        (mode_rows, shaped((128, NODES), BF)),
        (FAR,) * 3,
        (tile, tile, tile, rows, tile, rows, pltpu.SemaphoreType.DMA((3,))),
    )(newton_residual, inverse_blocks, iterate)
    pieces = over_mode(padded)

    held, slots, spots, ids = lax.optimization_barrier((held, slots, spots, neighbour_ids.T))
    (mine,) = call(turn_body, (shaped((4, K, 16, 128), BF),), (SMEM,) * 2 + (VMEM,) * 2, ())(
        side, ids, held, jnp.asarray(np.eye(128), BF)
    )
    theirs = lax.ppermute(mine, "elem", pairs_of(16, lambda i: i ^ 1))
    (coeffs,) = call(
        coefficient_body,
        (shaped((2, 96, 512), F32),),
        (SMEM,) + (ANY,) * 9,
        (
            pltpu.VMEM((8, ROWS, NODES), BF),
            pltpu.VMEM((480, NODES), F32),
            pltpu.VMEM((480, S), BF),
            pltpu.VMEM((S, 480), BF),
            pltpu.SemaphoreType.DMA((9,)),
        ),
    )(spots, *pieces, basis_values.T)

    gradients_of = jnp.asarray(gradient_table())
    own = jnp.asarray(own_tables())
    near = jnp.asarray(near_table())
    traces = jnp.asarray(trace_table())
    count = jnp.asarray(face_count())
    remainder = newton_residual
    for sweep in range(ITERS):
        along, toward, onward, grads = call(
            along_body,
            (
                shaped((2, ROWS, 512), BF),
                shaped((ROWS, 256), F32),
                shaped((ROWS, 256), F32),
                shaped((4, 16, 16, 512), BF),
            ),
            (SMEM, SMEM) + (ANY,) * 8 + (VMEM,) * 3 + (ANY,) * 3,
            (
                pltpu.VMEM((4, ROWS, NODES), BF),
                pltpu.VMEM((2, 16, 16, 512), BF),
                pltpu.SemaphoreType.DMA((4,)),
                pltpu.VMEM((256, 384), BF),
                pltpu.VMEM((MB, NODES), F32),
                pltpu.VMEM((2, 512, 128), BF),
                pltpu.SemaphoreType.DMA((3,)),
            ),
        )(slots, core, *pieces, mine, theirs, coeffs, gradients_of, correction, traces)
        after = lax.ppermute(toward, "elem", pairs_of(16, lambda i: (i + 15) % 16))
        before = lax.ppermute(onward, "elem", pairs_of(16, lambda i: (i + 1) % 16))
        (across,) = call(across_body, (shaped((4, ROWS, 512), BF),), (VMEM,) * 4, ())(
            mine, theirs, coeffs, grads
        )
        remainder, correction, padded = call(
            update_body,
            (mode_rows, mode_rows, padded_rows),
            (SMEM,) + (VMEM,) * 10,
            (tile, pltpu.VMEM((4, 16, ROWS, 128), F32), tile, tile, tile),
        )(ids, correction, along, across, before, after, newton_residual, inverse_blocks, own, near, count)
        pieces = over_mode(padded) if sweep + 1 < ITERS else None
    return (correction, remainder)


def solution(mesh):
    return jax.shard_map(
        per_device,
        mesh=mesh,
        in_specs=(
            P("mode", "elem"),
            P("mode", "elem"),
            P(None, "elem"),
            P(),
            P("mode", None, "elem"),
            P("mode", None),
            P("elem", None),
        ),
        out_specs=(P("mode", "elem"), P("mode", "elem")),
        check_vma=False,
    )
```

```python
import math

import jax
import jax.numpy as jnp
import numpy as np
from jax import lax
from jax.experimental import pallas as pl
from jax.experimental.pallas import tpu as pltpu
from jax.sharding import PartitionSpec as P

K = 84
S = 1024
ITERS = 2
MB = 60
ROWS = 64
NODES = 1024
PAIRS = 42
GROWTH = 0.5
TIME_STEP = 0.03
LIFT_SCALE = 6.0
PENALTY = 3.0
RELAX_WEIGHT = 0.8
FACE_OPPOSITE = (1, 0, 3, 2, 5, 4)
BF = jnp.bfloat16
F32 = jnp.float32
VMEM = pl.BlockSpec(memory_space=pltpu.VMEM)
SMEM = pl.BlockSpec(memory_space=pltpu.SMEM)
ANY = pl.BlockSpec(memory_space=pl.ANY)
FAR = pl.BlockSpec(memory_space=pltpu.HBM)


def line_derivative():
    inward = 1.0 / math.sqrt(5.0)
    points = np.array([-1.0, -inward, inward, 1.0])
    legendre = (5.0 * points**3 - 3.0 * points) / 2.0
    matrix = np.zeros((4, 4))
    for source in range(4):
        for target in range(4):
            if source != target:
                matrix[source, target] = legendre[source] / (
                    legendre[target] * (points[source] - points[target])
                )
    matrix[0, 0] = -3.0
    matrix[3, 3] = 3.0
    return matrix


def direction_tables():
    line_matrix = line_derivative()
    identity = np.eye(4)
    singles = [
        np.kron(np.kron(line_matrix, identity), identity),
        np.kron(np.kron(identity, line_matrix), identity),
        np.kron(np.kron(identity, identity), line_matrix),
    ]
    return [np.kron(np.eye(2), single).T.astype(np.float32) for single in singles]


def face_nodes():
    layout = np.arange(64).reshape(4, 4, 4)
    return [
        layout[:, 0, :].ravel(),
        layout[:, 3, :].ravel(),
        layout[:, :, 0].ravel(),
        layout[:, :, 3].ravel(),
        layout[0].ravel(),
        layout[3].ravel(),
    ]


def two_parts(table):
    high = np.asarray(table, np.float32).astype(jnp.bfloat16)
    low = (np.asarray(table, np.float32) - high.astype(np.float32)).astype(jnp.bfloat16)
    return high, low


def gradient_table():
    high, low = two_parts(np.concatenate(direction_tables(), axis=1))
    return np.concatenate([high, low], axis=0)


def own_tables():
    tables = direction_tables()
    nodes = face_nodes()
    result = []
    for axis, faces in enumerate(((4, 5), (0, 1), (2, 3))):
        table = tables[axis].copy()
        for sign, face in zip((-1.0, 1.0), faces):
            for node in nodes[face]:
                for half in (0, 64):
                    table[half + node, half + node] -= 0.5 * LIFT_SCALE * sign
        result.append(table)
    high, low = two_parts(np.concatenate(result, axis=0))
    return np.stack([high, low])


def near_table():
    nodes = face_nodes()
    table = np.zeros((256, 128), np.float32)
    for face in range(4):
        for source, target in zip(nodes[FACE_OPPOSITE[face]], nodes[face]):
            table[64 * face + source, target] = 1.0
            table[64 * face + source, 64 + target] = 1.0
    return table.astype(jnp.bfloat16)


def trace_table():
    table = np.zeros((2, 512, 128), np.float32)
    for element in range(8):
        for node in range(16):
            table[0, 64 * element + node, 16 * element + node] = 1.0
            table[1, 64 * element + 48 + node, 16 * element + node] = 1.0
    return table.astype(jnp.bfloat16)


def face_count():
    count = np.zeros((1, 128), np.float32)
    for nodes in face_nodes():
        for node in nodes:
            count[0, node] += 1.0
            count[0, 64 + node] += 1.0
    return count


def dot(left, right):
    return jnp.dot(left, right, preferred_element_type=F32)


def split(value):
    high = value.astype(BF)
    return high, (value - high.astype(F32)).astype(BF)


def call(body, outs, ins, scratch=(), limit=20 << 20):
    specs = [VMEM if isinstance(o, jax.ShapeDtypeStruct) else o for o in outs]
    return pl.pallas_call(
        body,
        out_shape=tuple(outs),
        in_specs=list(ins),
        out_specs=tuple(specs),
        scratch_shapes=list(scratch),
        compiler_params=pltpu.CompilerParams(vmem_limit_bytes=limit),
    )


def fetch(sources, targets, sem):
    copies = [
        pltpu.make_async_copy(source, target, sem.at[index])
        for index, (source, target) in enumerate(zip(sources, targets))
    ]
    for copy in copies:
        copy.start()
    return copies


def stored_body(x_ref, z_ref, wide, tall):
    wide[...] = jnp.zeros_like(wide)
    x = x_ref[...].astype(F32)
    wide[0:60, 0:1260] = x
    wide[64:124, 0:1259] = x[:, 1:]
    for block in range(10):
        tall[128 * block : 128 * block + 128, :] = wide[:, 128 * block : 128 * block + 128].T
    tall[1280:1344, :] = jnp.zeros((64, 128), F32)
    for pair in range(PAIRS):
        z_ref[pair] = tall[pl.ds(2 * pair, 16, stride=K), :].astype(BF)


def turn_body(side_ref, ids_ref, held, tt_ref):
    side = side_ref[0]
    place_row = lax.broadcasted_iota(jnp.int32, (128, 128), 0)
    place_column = lax.broadcasted_iota(jnp.int32, (128, 128), 1)
    eye = jnp.where(place_row == place_column, 1.0, 0.0).astype(BF)

    def step(twin, carry):
        rows = []
        for place in range(8):
            zone = side if place < 4 else 1 - side
            rows.append(held[place % 4, zone, pl.ds(2 * twin, 2)])
        both = jnp.concatenate([row[pair] for pair in range(2) for row in rows], axis=0)
        turned = lax.dot_general(
            eye, both, (((1,), (1,)), ((), ())), preferred_element_type=F32
        ).astype(BF)
        for pair in range(2):
            for half in range(2):
                for tile in range(4):
                    first = 64 * half + 16 * tile
                    tt_ref[tile, 4 * twin + 2 * pair + half] = turned[
                        first : first + 16, 128 * pair : 128 * pair + 128
                    ]
        return carry

    lax.fori_loop(0, PAIRS // 2, step, 0, unroll=3)


def coefficient_body(spot_ref, *refs):
    pieces, turned_ref, c_ref = refs[:8], refs[8], refs[9]
    low, joined, turned, basis, sem = refs[10:15]
    copies = fetch(
        [piece.at[64:128] for piece in pieces] + [turned_ref],
        [low.at[spot_ref[index]] for index in range(8)] + [turned],
        sem,
    )
    copies[8].wait()
    for block in range(8):
        rows = turned[:, 128 * block : 128 * block + 128].astype(F32).T
        basis[128 * block : 128 * block + 128, :] = rows.astype(BF)
    lead = turned[0:96, :]
    for copy in copies[:8]:
        copy.wait()
    for block in range(8):
        joined[60 * block : 60 * block + 60, :] = low[block].astype(F32)[0:60]
    for quarter in range(4):
        state = joined[:, 256 * quarter : 256 * quarter + 256].astype(BF)
        growth = jnp.exp(GROWTH * dot(basis[...], state))
        high, rest = split(growth)
        terms = (dot(lead, high) + dot(lead, rest)) * (1.0 / S)
        c_ref[quarter // 2, :, 256 * (quarter % 2) : 256 * (quarter % 2) + 256] = terms.astype(BF).astype(F32)


def invert(field, inv_ref, out_ref, base, weight):
    lane = lax.broadcasted_iota(jnp.int32, (64, 128), 1)
    first = lane < 64
    for pair in range(8):
        cols = slice(128 * pair, 128 * pair + 128)
        tile = inv_ref[:, cols]
        block = jnp.concatenate([jnp.where(first, tile, 0.0), jnp.where(first, 0.0, tile)], axis=0)
        high, low = split(block)
        fh, fl = split(field[:, cols])
        value = dot(fh, high) + dot(fl, high) + dot(fh, low)
        out_ref[:, cols] = value if base is None else base[:, cols] + weight * value


def pad_modes(value_ref, padded, wp_ref):
    padded[...] = jnp.zeros_like(padded)
    for group in range(4):
        padded[16 * group : 16 * group + 15, :] = value_ref[15 * group : 15 * group + 15, :]
    wp_ref[0:64, :] = padded[...].astype(BF)


def start_body(
    res_ref, inv_ref, state_ref, w_ref, wp_ref, field, value, padded, res, inverse, state, sem
):
    copies = fetch((state_ref, res_ref, inv_ref), (state, res, inverse), sem)
    field[60:64, :] = jnp.zeros((4, NODES), F32)
    copies[0].wait()
    field[0:60, :] = state[...]
    wp_ref[64:128, :] = field[...].astype(BF)
    copies[1].wait()
    field[0:60, :] = res[...]
    copies[2].wait()
    invert(field, inverse, value, None, None)
    w_ref[...] = value[0:60, :]
    pad_modes(value, padded, wp_ref)


def weighted(mine_ref, theirs_ref, grad, cf, half, out_ref, tile):
    for part in range(4):
        left = jnp.concatenate(
            [mine_ref[part].reshape(K * 16, 128), theirs_ref[part].reshape(K * 16, 128)], axis=1
        )
        terms = dot(left, grad)
        total = None
        for k in range(K):
            term = cf[half, k : k + 1, :] * terms[16 * k : 16 * k + 16]
            total = term if total is None else total + term
        out_ref[tile, 16 * part : 16 * part + 16, :] = total.astype(BF)


def along_body(slot_ref, core_ref, *refs):
    blocks = refs[0:8]
    mine_ref, theirs_ref, cf, table_src, w_src, trace_src = refs[8:14]
    f_ref, toward_ref, onward_ref, grads_ref = refs[14:18]
    picked, first_grads, sem, table_ref, w_ref, trace_ref, late = refs[18:25]
    copies = fetch((table_src, w_src, trace_src), (table_ref, w_ref, trace_ref), late)
    for stored in range(4):
        for index in range(8):

            @pl.when(slot_ref[stored] == index)
            def _(stored=stored, index=index):
                pltpu.make_async_copy(
                    blocks[index].at[0:64], picked.at[stored], sem.at[stored]
                ).start()

    for stored in range(4):
        pltpu.make_async_copy(blocks[0].at[0:64], picked.at[stored], sem.at[stored]).wait()
    core = core_ref[0]
    copies[0].wait()
    for pair in range(8):
        tile = picked[:, :, 128 * pair : 128 * pair + 128].reshape(256, 128)
        values = dot(jnp.concatenate([tile, tile], axis=1), table_ref[...]).astype(BF)
        cols = slice(128 * (pair % 4), 128 * (pair % 4) + 128)
        for source in range(16):
            spot = (source // 2) + 8 * (core if source % 2 == 0 else 1 - core)
            for axis in range(3):
                rows = values[16 * source : 16 * source + 16, 128 * axis : 128 * axis + 128]
                if axis == 0:
                    first_grads[pair // 4, spot, :, cols] = rows
                else:
                    grads_ref[2 * (axis - 1) + pair // 4, spot, :, cols] = rows

    def step(half, carry):
        grad = first_grads[half].reshape(256, 512)
        weighted(mine_ref, theirs_ref, grad, cf, half, f_ref, half)
        return carry

    lax.fori_loop(0, 2, step, 0)
    copies[1].wait()
    copies[2].wait()
    zero = jnp.zeros((4, 512), F32)
    for half in range(2):
        value = (LIFT_SCALE * PENALTY) * jnp.concatenate(
            [w_ref[:, 512 * half : 512 * half + 512], zero], axis=0
        )
        flux = (0.5 * LIFT_SCALE) * f_ref[half].astype(F32)
        for table, mixed, out_ref in (
            (trace_ref[0], value + flux, toward_ref),
            (trace_ref[1], value - flux, onward_ref),
        ):
            high, low = split(mixed)
            out_ref[:, 128 * half : 128 * half + 128] = dot(high, table) + dot(low, table)


def across_body(mine_ref, theirs_ref, cf, grads_ref, f_ref):
    def step(tile, carry):
        grad = grads_ref[tile].reshape(256, 512)
        weighted(mine_ref, theirs_ref, grad, cf, lax.rem(tile, 2), f_ref, tile)
        return carry

    lax.fori_loop(0, 4, step, 0)


def update_body(
    ids_ref, w_ref, fx_ref, f_ref, up_ref, un_ref, res_ref, inv_ref, own_ref, near_ref, count_ref,
    rem_ref, corr_ref, wp_ref, v, faces, rem, value, padded,
):
    lane = lax.broadcasted_iota(jnp.int32, (64, 128), 1)
    first = lane < 64
    v[60:64, :] = jnp.zeros((4, NODES), F32)
    v[0:60, :] = w_ref[...]
    rem[60:64, :] = jnp.zeros((4, NODES), F32)
    rem[0:60, :] = res_ref[...]

    def flux(axis, pair):
        source, index = (fx_ref, pair // 4) if axis == 0 else (f_ref, 2 * (axis - 1) + pair // 4)
        return source[index, :, 128 * (pair % 4) : 128 * (pair % 4) + 128]

    for pair in range(8):
        scaled = (LIFT_SCALE * PENALTY) * v[:, 128 * pair : 128 * pair + 128]
        for axis in (1, 2):
            part = (0.5 * LIFT_SCALE) * flux(axis, pair).astype(F32)
            for side, mixed in enumerate((scaled - part, scaled + part)):
                face = 2 * (axis - 1) + side
                turned = pltpu.roll(mixed, 64, axis=1)
                faces[face, 2 * pair] = jnp.where(first, mixed, turned)
                faces[face, 2 * pair + 1] = jnp.where(first, turned, mixed)
    near = []
    for element in range(16):
        left = jnp.where(first, faces[0, ids_ref[0, element]], faces[1, ids_ref[1, element]])
        right = jnp.where(first, faces[2, ids_ref[2, element]], faces[3, ids_ref[3, element]])
        high, low = split(jnp.concatenate([left, right], axis=1))
        near.append(dot(high, near_ref[...]) + dot(low, near_ref[...]))
    row = lax.broadcasted_iota(jnp.int32, (256, 128), 0)
    column = lax.broadcasted_iota(jnp.int32, (1, 128), 1)
    inner = column % 64
    uh, ul = split(up_ref[...])
    nh, nl = split(un_ref[...])
    for pair in range(8):
        cols = slice(128 * pair, 128 * pair + 128)
        left, right = 2 * pair, 2 * pair + 1
        below = 16 * jnp.where(column < 64, ids_ref[4, left], ids_ref[4, right]) + inner
        above = 16 * jnp.where(column < 64, ids_ref[5, left], ids_ref[5, right]) + inner - 48
        lower = jnp.where(row == jnp.where(inner < 16, below, -1), 1.0, 0.0).astype(BF)
        upper = jnp.where(row == jnp.where(inner >= 48, above, -1), 1.0, 0.0).astype(BF)
        across = dot(uh, lower) + dot(ul, lower) + dot(nh, upper) + dot(nl, upper)
        joined = jnp.concatenate([flux(axis, pair) for axis in range(3)], axis=1)
        inside = dot(joined, own_ref[0]) + dot(joined, own_ref[1])
        here = v[:, cols]
        divergence = (
            inside
            + jnp.where(first, near[2 * pair], near[2 * pair + 1])
            + across
            - (LIFT_SCALE * PENALTY) * count_ref[...] * here
        )
        rem[:, cols] = rem[:, cols] - (here - TIME_STEP * divergence)
    invert(rem, inv_ref, value, v, RELAX_WEIGHT)
    rem_ref[...] = rem[0:60, :]
    corr_ref[...] = value[0:60, :]
    pad_modes(value, padded, wp_ref)


def shaped(shape, dtype):
    return jax.ShapeDtypeStruct(shape, dtype)


def pairs_of(count, move):
    return [(index, move(index)) for index in range(count)]


def over_mode(block):
    def along(step):
        return pairs_of(8, lambda i: ((i // 2 + step) % 4) * 2 + i % 2)

    flip = pairs_of(8, lambda i: i ^ 1)
    other = lax.ppermute(block, "mode", flip)
    one = lax.ppermute(block, "mode", along(1))
    two = lax.ppermute(block, "mode", along(2))
    three = lax.ppermute(block, "mode", along(3))
    return [
        block,
        one,
        two,
        three,
        other,
        lax.ppermute(other, "mode", along(1)),
        lax.ppermute(two, "mode", flip),
        lax.ppermute(three, "mode", flip),
    ]


def per_device(
    iterate,
    newton_residual,
    inverse_blocks,
    basis_values,
    triple_blocks,
    block_columns,
    neighbour_ids,
):
    mode = lax.axis_index("mode")
    elem = lax.axis_index("elem")
    steps = jnp.arange(8, dtype=jnp.int32)
    spots = ((mode // 2 - steps % 4) % 4) * 2 + ((mode % 2) ^ (steps // 4))
    columns = block_columns[0]
    slots = (mode // 2 - columns // 2) % 4 + 4 * ((mode % 2) ^ (columns % 2))
    core = (elem & 1)[None]
    side = (elem // 8)[None]
    mode_rows = shaped((MB, NODES), F32)
    padded_rows = shaped((ROWS, NODES), BF)
    tile = pltpu.VMEM((ROWS, NODES), F32)
    rows = pltpu.VMEM((MB, NODES), F32)

    (stored,) = call(
        stored_body,
        (shaped((PAIRS, 16, 128), BF),),
        (VMEM,),
        (pltpu.VMEM((128, 1280), F32), pltpu.VMEM((1344, 128), F32)),
    )(triple_blocks.reshape(MB, 1260))
    far = lax.ppermute(stored, "elem", pairs_of(16, lambda i: i ^ 8))
    groups = [[8 * zone + 2 * y + c for y in range(4)] for zone in range(2) for c in range(2)]
    sent = jnp.broadcast_to(jnp.stack([stored, far]), (4, 2, PAIRS, 16, 128))
    held = lax.all_to_all(sent, "elem", 0, 0, axis_index_groups=groups)
    correction, padded = call(
        start_body,
        (mode_rows, shaped((128, NODES), BF)),
        (FAR,) * 3,
        (tile, tile, tile, rows, tile, rows, pltpu.SemaphoreType.DMA((3,))),
        56 << 20,
    )(newton_residual, inverse_blocks, iterate)
    pieces = over_mode(padded)

    held, slots, spots, ids = lax.optimization_barrier((held, slots, spots, neighbour_ids.T))
    (mine,) = call(turn_body, (shaped((4, K, 16, 128), BF),), (SMEM,) * 2 + (VMEM,), ())(
        side, ids, held
    )
    theirs = lax.ppermute(mine, "elem", pairs_of(16, lambda i: i ^ 1))
    (coeffs,) = call(
        coefficient_body,
        (shaped((2, 96, 512), F32),),
        (SMEM,) + (ANY,) * 9,
        (
            pltpu.VMEM((8, ROWS, NODES), BF),
            pltpu.VMEM((480, NODES), F32),
            pltpu.VMEM((480, S), BF),
            pltpu.VMEM((S, 480), BF),
            pltpu.SemaphoreType.DMA((9,)),
        ),
    )(spots, *pieces, basis_values.T)

    gradients_of = jnp.asarray(gradient_table())
    own = jnp.asarray(own_tables())
    near = jnp.asarray(near_table())
    traces = jnp.asarray(trace_table())
    count = jnp.asarray(face_count())
    remainder = newton_residual
    for sweep in range(ITERS):
        along, toward, onward, grads = call(
            along_body,
            (
                shaped((2, ROWS, 512), BF),
                shaped((ROWS, 256), F32),
                shaped((ROWS, 256), F32),
                shaped((4, 16, 16, 512), BF),
            ),
            (SMEM, SMEM) + (ANY,) * 8 + (VMEM,) * 3 + (ANY,) * 3,
            (
                pltpu.VMEM((4, ROWS, NODES), BF),
                pltpu.VMEM((2, 16, 16, 512), BF),
                pltpu.SemaphoreType.DMA((4,)),
                pltpu.VMEM((256, 384), BF),
                pltpu.VMEM((MB, NODES), F32),
                pltpu.VMEM((2, 512, 128), BF),
                pltpu.SemaphoreType.DMA((3,)),
            ),
        )(slots, core, *pieces, mine, theirs, coeffs, gradients_of, correction, traces)
        after = lax.ppermute(toward, "elem", pairs_of(16, lambda i: (i + 15) % 16))
        before = lax.ppermute(onward, "elem", pairs_of(16, lambda i: (i + 1) % 16))
        (across,) = call(across_body, (shaped((4, ROWS, 512), BF),), (VMEM,) * 4, ())(
            mine, theirs, coeffs, grads
        )
        remainder, correction, padded = call(
            update_body,
            (mode_rows, mode_rows, padded_rows),
            (SMEM,) + (VMEM,) * 10,
            (tile, pltpu.VMEM((4, 16, ROWS, 128), F32), tile, tile, tile),
        )(ids, correction, along, across, before, after, newton_residual, inverse_blocks, own, near, count)
        pieces = over_mode(padded) if sweep + 1 < ITERS else None
    return (correction, remainder)


def solution(mesh):
    return jax.shard_map(
        per_device,
        mesh=mesh,
        in_specs=(
            P("mode", "elem"),
            P("mode", "elem"),
            P(None, "elem"),
            P(),
            P("mode", None, "elem"),
            P("mode", None),
            P("elem", None),
        ),
        out_specs=(P("mode", "elem"), P("mode", "elem")),
        check_vma=False,
    )
```

```python
import math

import jax
import jax.numpy as jnp
import numpy as np
from jax import lax
from jax.experimental import pallas as pl
from jax.experimental.pallas import tpu as pltpu
from jax.sharding import PartitionSpec as P

K = 84
S = 1024
ITERS = 2
MB = 60
ROWS = 64
NODES = 1024
PAIRS = 42
GROWTH = 0.5
TIME_STEP = 0.03
LIFT_SCALE = 6.0
PENALTY = 3.0
RELAX_WEIGHT = 0.8
FACE_OPPOSITE = (1, 0, 3, 2, 5, 4)
BF = jnp.bfloat16
F32 = jnp.float32
VMEM = pl.BlockSpec(memory_space=pltpu.VMEM)
SMEM = pl.BlockSpec(memory_space=pltpu.SMEM)
ANY = pl.BlockSpec(memory_space=pl.ANY)
FAR = pl.BlockSpec(memory_space=pltpu.HBM)


def line_derivative():
    inward = 1.0 / math.sqrt(5.0)
    points = np.array([-1.0, -inward, inward, 1.0])
    legendre = (5.0 * points**3 - 3.0 * points) / 2.0
    matrix = np.zeros((4, 4))
    for source in range(4):
        for target in range(4):
            if source != target:
                matrix[source, target] = legendre[source] / (
                    legendre[target] * (points[source] - points[target])
                )
    matrix[0, 0] = -3.0
    matrix[3, 3] = 3.0
    return matrix


def direction_tables():
    line_matrix = line_derivative()
    identity = np.eye(4)
    singles = [
        np.kron(np.kron(line_matrix, identity), identity),
        np.kron(np.kron(identity, line_matrix), identity),
        np.kron(np.kron(identity, identity), line_matrix),
    ]
    return [np.kron(np.eye(2), single).T.astype(np.float32) for single in singles]


def face_nodes():
    layout = np.arange(64).reshape(4, 4, 4)
    return [
        layout[:, 0, :].ravel(),
        layout[:, 3, :].ravel(),
        layout[:, :, 0].ravel(),
        layout[:, :, 3].ravel(),
        layout[0].ravel(),
        layout[3].ravel(),
    ]


def two_parts(table):
    high = np.asarray(table, np.float32).astype(jnp.bfloat16)
    low = (np.asarray(table, np.float32) - high.astype(np.float32)).astype(jnp.bfloat16)
    return high, low


def gradient_table():
    high, low = two_parts(np.concatenate(direction_tables(), axis=1))
    return np.concatenate([high, low], axis=0)


def own_tables():
    tables = direction_tables()
    nodes = face_nodes()
    result = []
    for axis, faces in enumerate(((4, 5), (0, 1), (2, 3))):
        table = tables[axis].copy()
        for sign, face in zip((-1.0, 1.0), faces):
            for node in nodes[face]:
                for half in (0, 64):
                    table[half + node, half + node] -= 0.5 * LIFT_SCALE * sign
        result.append(table)
    high, low = two_parts(np.concatenate(result, axis=0))
    return np.stack([high, low])


def near_table():
    nodes = face_nodes()
    table = np.zeros((256, 128), np.float32)
    for face in range(4):
        for source, target in zip(nodes[FACE_OPPOSITE[face]], nodes[face]):
            table[64 * face + source, target] = 1.0
            table[64 * face + source, 64 + target] = 1.0
    return table.astype(jnp.bfloat16)


def trace_table():
    table = np.zeros((2, 512, 128), np.float32)
    for element in range(8):
        for node in range(16):
            table[0, 64 * element + node, 16 * element + node] = 1.0
            table[1, 64 * element + 48 + node, 16 * element + node] = 1.0
    return table.astype(jnp.bfloat16)


def face_count():
    count = np.zeros((1, 128), np.float32)
    for nodes in face_nodes():
        for node in nodes:
            count[0, node] += 1.0
            count[0, 64 + node] += 1.0
    return count


def dot(left, right):
    return jnp.dot(left, right, preferred_element_type=F32)


def split(value):
    high = value.astype(BF)
    return high, (value - high.astype(F32)).astype(BF)


def call(body, outs, ins, scratch=(), limit=20 << 20):
    specs = [VMEM if isinstance(o, jax.ShapeDtypeStruct) else o for o in outs]
    return pl.pallas_call(
        body,
        out_shape=tuple(outs),
        in_specs=list(ins),
        out_specs=tuple(specs),
        scratch_shapes=list(scratch),
        compiler_params=pltpu.CompilerParams(vmem_limit_bytes=limit),
    )


def fetch(sources, targets, sem):
    copies = [
        pltpu.make_async_copy(source, target, sem.at[index])
        for index, (source, target) in enumerate(zip(sources, targets))
    ]
    for copy in copies:
        copy.start()
    return copies


def stored_body(x_ref, z_ref, wide, tall):
    wide[...] = jnp.zeros_like(wide)
    x = x_ref[...].astype(F32)
    wide[0:60, 0:1260] = x
    wide[64:124, 0:1259] = x[:, 1:]
    for block in range(10):
        tall[128 * block : 128 * block + 128, :] = wide[:, 128 * block : 128 * block + 128].T
    tall[1280:1344, :] = jnp.zeros((64, 128), F32)
    for pair in range(PAIRS):
        z_ref[pair] = tall[pl.ds(2 * pair, 16, stride=K), :].astype(BF)


def turn_body(side_ref, ids_ref, held, tt_ref):
    side = side_ref[0]
    place_row = lax.broadcasted_iota(jnp.int32, (128, 128), 0)
    place_column = lax.broadcasted_iota(jnp.int32, (128, 128), 1)
    half, group, inner = (place_row // 4) % 2, place_row // 8, place_row % 4
    order = jnp.where(place_column == 64 * half + 4 * group + inner, 1.0, 0.0).astype(BF)

    def step(twin, carry):
        rows = []
        for place in range(8):
            zone = side if place < 4 else 1 - side
            rows.append(held[place % 4, zone, pl.ds(2 * twin, 2)])
        both = jnp.concatenate([row[pair] for pair in range(2) for row in rows], axis=0)
        turned = lax.dot_general(
            order, both, (((1,), (1,)), ((), ())), preferred_element_type=F32
        )
        for group in range(15):
            rows = slice(8 * group, 8 * group + 8)
            pair = jnp.concatenate([turned[rows, 0:128], turned[rows, 128:256]], axis=0)
            tt_ref[group, twin] = pair.astype(BF)
        return carry

    lax.fori_loop(0, PAIRS // 2, step, 0, unroll=7)


def coefficient_body(spot_ref, *refs):
    pieces, turned_ref, c_ref = refs[:8], refs[8], refs[9]
    low, joined, turned, basis, sem = refs[10:15]
    copies = fetch(
        [piece.at[64:128] for piece in pieces] + [turned_ref],
        [low.at[spot_ref[index]] for index in range(8)] + [turned],
        sem,
    )
    copies[8].wait()
    for block in range(8):
        rows = turned[:, 128 * block : 128 * block + 128].astype(F32).T
        basis[128 * block : 128 * block + 128, :] = rows.astype(BF)
    lead = turned[0:96, :]
    for copy in copies[:8]:
        copy.wait()
    for block in range(8):
        joined[60 * block : 60 * block + 60, :] = low[block].astype(F32)[0:60]
    upper = lax.broadcasted_iota(jnp.int32, (8, 256), 0) < 4
    for quarter in range(4):
        state = joined[:, 256 * quarter : 256 * quarter + 256].astype(BF)
        growth = jnp.exp(GROWTH * dot(basis[...], state))
        high, rest = split(growth)
        terms = (dot(lead, high) + dot(lead, rest)) * (1.0 / S)
        terms = terms.astype(BF).astype(F32)
        for pair in range(PAIRS):
            c_ref[quarter // 2, pair, :, 256 * (quarter % 2) : 256 * (quarter % 2) + 256] = jnp.where(
                upper, terms[2 * pair : 2 * pair + 1], terms[2 * pair + 1 : 2 * pair + 2]
            )


def invert(field, inv_ref, out_ref, base, weight):
    lane = lax.broadcasted_iota(jnp.int32, (64, 128), 1)
    first = lane < 64
    for pair in range(8):
        cols = slice(128 * pair, 128 * pair + 128)
        tile = inv_ref[:, cols]
        block = jnp.concatenate([jnp.where(first, tile, 0.0), jnp.where(first, 0.0, tile)], axis=0)
        high, low = split(block)
        fh, fl = split(field[:, cols])
        value = dot(fh, high) + dot(fl, high) + dot(fh, low)
        out_ref[:, cols] = value if base is None else base[:, cols] + weight * value


def pad_modes(value_ref, padded, wp_ref):
    padded[...] = jnp.zeros_like(padded)
    for group in range(4):
        padded[16 * group : 16 * group + 15, :] = value_ref[15 * group : 15 * group + 15, :]
    wp_ref[0:64, :] = padded[...].astype(BF)


def start_body(
    res_ref, inv_ref, state_ref, w_ref, wp_ref, field, value, padded, res, inverse, state, sem
):
    copies = fetch((state_ref, res_ref, inv_ref), (state, res, inverse), sem)
    field[60:64, :] = jnp.zeros((4, NODES), F32)
    copies[0].wait()
    field[0:60, :] = state[...]
    wp_ref[64:128, :] = field[...].astype(BF)
    copies[1].wait()
    field[0:60, :] = res[...]
    copies[2].wait()
    invert(field, inverse, value, None, None)
    w_ref[...] = value[0:60, :]
    pad_modes(value, padded, wp_ref)


def weighted(mine_ref, theirs_ref, grad, cf, half, out_ref, tile, whole):
    for block in range(5):
        rows = slice(3 * block, 3 * block + 3)
        left = jnp.concatenate(
            [mine_ref[rows].reshape(24 * PAIRS, 128), theirs_ref[rows].reshape(24 * PAIRS, 128)], axis=1
        )
        terms = dot(left, grad)
        for inner in range(3):
            total = None
            for pair in range(PAIRS):
                first = 8 * (PAIRS * inner + pair)
                term = cf[half, pair] * terms[first : first + 8]
                total = term if total is None else total + term
            group = 3 * block + inner
            whole[4 * group : 4 * group + 4, :] = total[0:4] + total[4:8]
    out_ref[tile] = whole[...].astype(BF)


def along_body(slot_ref, core_ref, *refs):
    blocks = refs[0:8]
    mine_ref, theirs_ref, cf, table_src, w_src, trace_src = refs[8:14]
    f_ref, toward_ref, onward_ref, grads_ref = refs[14:18]
    picked, first_grads, sem, table_ref, w_ref, trace_ref, late, whole = refs[18:26]
    whole[60:64, :] = jnp.zeros((4, 512), F32)
    copies = fetch((table_src, w_src, trace_src), (table_ref, w_ref, trace_ref), late)
    for stored in range(4):
        for index in range(8):

            @pl.when(slot_ref[stored] == index)
            def _(stored=stored, index=index):
                pltpu.make_async_copy(
                    blocks[index].at[0:64], picked.at[stored], sem.at[stored]
                ).start()

    for stored in range(4):
        pltpu.make_async_copy(blocks[0].at[0:64], picked.at[stored], sem.at[stored]).wait()
    core = core_ref[0]
    copies[0].wait()
    for pair in range(8):
        tile = picked[:, :, 128 * pair : 128 * pair + 128].reshape(256, 128)
        values = dot(jnp.concatenate([tile, tile], axis=1), table_ref[...]).astype(BF)
        cols = slice(128 * (pair % 4), 128 * (pair % 4) + 128)
        for source in range(16):
            spot = (source // 2) + 8 * (core if source % 2 == 0 else 1 - core)
            for axis in range(3):
                rows = values[16 * source : 16 * source + 16, 128 * axis : 128 * axis + 128]
                if axis == 0:
                    first_grads[pair // 4, spot, :, cols] = rows
                else:
                    grads_ref[2 * (axis - 1) + pair // 4, spot, :, cols] = rows

    def step(half, carry):
        grad = first_grads[half].reshape(256, 512)
        weighted(mine_ref, theirs_ref, grad, cf, half, f_ref, half, whole)
        return carry

    lax.fori_loop(0, 2, step, 0)
    copies[1].wait()
    copies[2].wait()
    zero = jnp.zeros((4, 512), F32)
    for half in range(2):
        value = (LIFT_SCALE * PENALTY) * jnp.concatenate(
            [w_ref[:, 512 * half : 512 * half + 512], zero], axis=0
        )
        flux = (0.5 * LIFT_SCALE) * f_ref[half].astype(F32)
        for table, mixed, out_ref in (
            (trace_ref[0], value + flux, toward_ref),
            (trace_ref[1], value - flux, onward_ref),
        ):
            high, low = split(mixed)
            out_ref[:, 128 * half : 128 * half + 128] = dot(high, table) + dot(low, table)


def across_body(mine_ref, theirs_ref, cf, grads_ref, f_ref, whole):
    whole[60:64, :] = jnp.zeros((4, 512), F32)

    def step(tile, carry):
        grad = grads_ref[tile].reshape(256, 512)
        weighted(mine_ref, theirs_ref, grad, cf, lax.rem(tile, 2), f_ref, tile, whole)
        return carry

    lax.fori_loop(0, 4, step, 0)


def update_body(
    ids_ref, w_ref, fx_ref, f_ref, up_ref, un_ref, res_ref, inv_ref, own_ref, near_ref, count_ref,
    rem_ref, corr_ref, wp_ref, v, faces, rem, value, padded,
):
    lane = lax.broadcasted_iota(jnp.int32, (64, 128), 1)
    first = lane < 64
    v[60:64, :] = jnp.zeros((4, NODES), F32)
    v[0:60, :] = w_ref[...]
    rem[60:64, :] = jnp.zeros((4, NODES), F32)
    rem[0:60, :] = res_ref[...]

    def flux(axis, pair):
        source, index = (fx_ref, pair // 4) if axis == 0 else (f_ref, 2 * (axis - 1) + pair // 4)
        return source[index, :, 128 * (pair % 4) : 128 * (pair % 4) + 128]

    for pair in range(8):
        scaled = (LIFT_SCALE * PENALTY) * v[:, 128 * pair : 128 * pair + 128]
        for axis in (1, 2):
            part = (0.5 * LIFT_SCALE) * flux(axis, pair).astype(F32)
            for side, mixed in enumerate((scaled - part, scaled + part)):
                face = 2 * (axis - 1) + side
                turned = pltpu.roll(mixed, 64, axis=1)
                faces[face, 2 * pair] = jnp.where(first, mixed, turned)
                faces[face, 2 * pair + 1] = jnp.where(first, turned, mixed)
    near = []
    for element in range(16):
        left = jnp.where(first, faces[0, ids_ref[0, element]], faces[1, ids_ref[1, element]])
        right = jnp.where(first, faces[2, ids_ref[2, element]], faces[3, ids_ref[3, element]])
        high, low = split(jnp.concatenate([left, right], axis=1))
        near.append(dot(high, near_ref[...]) + dot(low, near_ref[...]))
    row = lax.broadcasted_iota(jnp.int32, (256, 128), 0)
    column = lax.broadcasted_iota(jnp.int32, (1, 128), 1)
    inner = column % 64
    uh, ul = split(up_ref[...])
    nh, nl = split(un_ref[...])
    for pair in range(8):
        cols = slice(128 * pair, 128 * pair + 128)
        left, right = 2 * pair, 2 * pair + 1
        below = 16 * jnp.where(column < 64, ids_ref[4, left], ids_ref[4, right]) + inner
        above = 16 * jnp.where(column < 64, ids_ref[5, left], ids_ref[5, right]) + inner - 48
        lower = jnp.where(row == jnp.where(inner < 16, below, -1), 1.0, 0.0).astype(BF)
        upper = jnp.where(row == jnp.where(inner >= 48, above, -1), 1.0, 0.0).astype(BF)
        across = dot(uh, lower) + dot(ul, lower) + dot(nh, upper) + dot(nl, upper)
        joined = jnp.concatenate([flux(axis, pair) for axis in range(3)], axis=1)
        inside = dot(joined, own_ref[0]) + dot(joined, own_ref[1])
        here = v[:, cols]
        divergence = (
            inside
            + jnp.where(first, near[2 * pair], near[2 * pair + 1])
            + across
            - (LIFT_SCALE * PENALTY) * count_ref[...] * here
        )
        rem[:, cols] = rem[:, cols] - (here - TIME_STEP * divergence)
    invert(rem, inv_ref, value, v, RELAX_WEIGHT)
    rem_ref[...] = rem[0:60, :]
    corr_ref[...] = value[0:60, :]
    pad_modes(value, padded, wp_ref)


def shaped(shape, dtype):
    return jax.ShapeDtypeStruct(shape, dtype)


def pairs_of(count, move):
    return [(index, move(index)) for index in range(count)]


def over_mode(block):
    def along(step):
        return pairs_of(8, lambda i: ((i // 2 + step) % 4) * 2 + i % 2)

    flip = pairs_of(8, lambda i: i ^ 1)
    other = lax.ppermute(block, "mode", flip)
    one = lax.ppermute(block, "mode", along(1))
    two = lax.ppermute(block, "mode", along(2))
    three = lax.ppermute(block, "mode", along(3))
    return [
        block,
        one,
        two,
        three,
        other,
        lax.ppermute(other, "mode", along(1)),
        lax.ppermute(two, "mode", flip),
        lax.ppermute(three, "mode", flip),
    ]


def per_device(
    iterate,
    newton_residual,
    inverse_blocks,
    basis_values,
    triple_blocks,
    block_columns,
    neighbour_ids,
):
    mode = lax.axis_index("mode")
    elem = lax.axis_index("elem")
    steps = jnp.arange(8, dtype=jnp.int32)
    spots = ((mode // 2 - steps % 4) % 4) * 2 + ((mode % 2) ^ (steps // 4))
    columns = block_columns[0]
    slots = (mode // 2 - columns // 2) % 4 + 4 * ((mode % 2) ^ (columns % 2))
    core = (elem & 1)[None]
    side = (elem // 8)[None]
    mode_rows = shaped((MB, NODES), F32)
    padded_rows = shaped((ROWS, NODES), BF)
    tile = pltpu.VMEM((ROWS, NODES), F32)
    rows = pltpu.VMEM((MB, NODES), F32)

    (stored,) = call(
        stored_body,
        (shaped((PAIRS, 16, 128), BF),),
        (VMEM,),
        (pltpu.VMEM((128, 1280), F32), pltpu.VMEM((1344, 128), F32)),
    )(triple_blocks.reshape(MB, 1260))
    far = lax.ppermute(stored, "elem", pairs_of(16, lambda i: i ^ 8))
    groups = [[8 * zone + 2 * y + c for y in range(4)] for zone in range(2) for c in range(2)]
    sent = jnp.broadcast_to(jnp.stack([stored, far]), (4, 2, PAIRS, 16, 128))
    held = lax.all_to_all(sent, "elem", 0, 0, axis_index_groups=groups)
    correction, padded = call(
        start_body,
        (mode_rows, shaped((128, NODES), BF)),
        (FAR,) * 3,
        (tile, tile, tile, rows, tile, rows, pltpu.SemaphoreType.DMA((3,))),
        56 << 20,
    )(newton_residual, inverse_blocks, iterate)
    pieces = over_mode(padded)

    held, slots, spots, ids = lax.optimization_barrier((held, slots, spots, neighbour_ids.T))
    (mine,) = call(turn_body, (shaped((15, PAIRS // 2, 16, 128), BF),), (SMEM,) * 2 + (VMEM,), ())(
        side, ids, held
    )
    theirs = lax.ppermute(mine, "elem", pairs_of(16, lambda i: i ^ 1))
    (coeffs,) = call(
        coefficient_body,
        (shaped((2, PAIRS, 8, 512), F32),),
        (SMEM,) + (ANY,) * 9,
        (
            pltpu.VMEM((8, ROWS, NODES), BF),
            pltpu.VMEM((480, NODES), F32),
            pltpu.VMEM((480, S), BF),
            pltpu.VMEM((S, 480), BF),
            pltpu.SemaphoreType.DMA((9,)),
        ),
    )(spots, *pieces, basis_values.T)

    gradients_of = jnp.asarray(gradient_table())
    own = jnp.asarray(own_tables())
    near = jnp.asarray(near_table())
    traces = jnp.asarray(trace_table())
    count = jnp.asarray(face_count())
    remainder = newton_residual
    for sweep in range(ITERS):
        along, toward, onward, grads = call(
            along_body,
            (
                shaped((2, ROWS, 512), BF),
                shaped((ROWS, 256), F32),
                shaped((ROWS, 256), F32),
                shaped((4, 16, 16, 512), BF),
            ),
            (SMEM, SMEM) + (ANY,) * 8 + (VMEM,) * 3 + (ANY,) * 3,
            (
                pltpu.VMEM((4, ROWS, NODES), BF),
                pltpu.VMEM((2, 16, 16, 512), BF),
                pltpu.SemaphoreType.DMA((4,)),
                pltpu.VMEM((256, 384), BF),
                pltpu.VMEM((MB, NODES), F32),
                pltpu.VMEM((2, 512, 128), BF),
                pltpu.SemaphoreType.DMA((3,)),
                pltpu.VMEM((ROWS, 512), F32),
            ),
        )(slots, core, *pieces, mine, theirs, coeffs, gradients_of, correction, traces)
        after = lax.ppermute(toward, "elem", pairs_of(16, lambda i: (i + 15) % 16))
        before = lax.ppermute(onward, "elem", pairs_of(16, lambda i: (i + 1) % 16))
        (across,) = call(across_body, (shaped((4, ROWS, 512), BF),), (VMEM,) * 4, (pltpu.VMEM((ROWS, 512), F32),))(
            mine, theirs, coeffs, grads
        )
        remainder, correction, padded = call(
            update_body,
            (mode_rows, mode_rows, padded_rows),
            (SMEM,) + (VMEM,) * 10,
            (tile, pltpu.VMEM((4, 16, ROWS, 128), F32), tile, tile, tile),
        )(ids, correction, along, across, before, after, newton_residual, inverse_blocks, own, near, count)
        pieces = over_mode(padded) if sweep + 1 < ITERS else None
    return (correction, remainder)


def solution(mesh):
    return jax.shard_map(
        per_device,
        mesh=mesh,
        in_specs=(
            P("mode", "elem"),
            P("mode", "elem"),
            P(None, "elem"),
            P(),
            P("mode", None, "elem"),
            P("mode", None),
            P("elem", None),
        ),
        out_specs=(P("mode", "elem"), P("mode", "elem")),
        check_vma=False,
    )
```
